32 devices in a mesh: groups: 1, pts: 32 (over z, y, x, core).
Axes of the slice: x: 2, y: 2, z: 4, core: 2. Of those that a mesh axis runs over, the one named last changes fastest.
Arguments:
- residual_cols: bfloat16 [16384, 256], P(('groups', 'pts')), may hold values from -6 to 6
- leaf_inverse: bfloat16 [16384, 128], P(('groups', 'pts'))
- basis_left: float32 [7, 16384, 128], P(None, ('groups', 'pts')), may hold values from -0.15625 to 0.15625
- basis_right: float32 [7, 16384, 128], P(None, ('groups', 'pts'))
- point_pos: float32 [16384], replicated, may hold values from 0 to 16, as said below
- map_pos: float32 [2048], P('pts'), may hold values from 0 to 16, as said below
- prior_map: bfloat16 [2048, 256], P(('groups', 'pts')), may hold values from -6 to 6
- block_first: int32 [32, 32], replicated, may hold values from 0 to 2, as said below
- block_count: int32 [32, 32], replicated, may hold values from 0 to 2, as said below
Outputs:
- solved_cols: float32 [16384, 256], P(('groups', 'pts'))
- sample_map: float32 [2048, 256], P(('groups', 'pts'))
The draws below stay inside these ranges and needn't reach their ends.
Inputs may be any that keep to these rules, and one draw needn't show every extreme that they name: `block_count`: at most 2; the listed blocks of tile d from source s include every block of s that has a point within distance 1 of some map point of tile d; in every draw some tile owner receives 2 blocks from every source; the totals per owner differ strongly between owners. `block_first`: listed blocks stay inside the source's 4 blocks. `point_pos`: points of one leaf block lie in increasing order within an interval of length 1. `map_pos`: the map points of one tile lie within an interval of length at most 6.
All inputs are finite; a program needn't handle non-finite values.
Results may differ from the reference program's by a relative error of at most 0.003.
Values may be sent and summed in bfloat16 or wider, within the bound.
A program may use at most 128 MiB of HBM per device.

```python
import jax
import jax.numpy as jnp
from jax import lax

MAP_DEV = 64
SAMPLES = 256
RANK = 128
LEAF = 128
LEVELS = 7
CAP = 2
BLK_DEV = 4
POINTS = 16384
MAPS = 2048
N_PTS = 32


def draw_leaf_inverse(key, part):
    first_key, second_key = jax.random.split(key)
    row_place = jnp.arange(POINTS)[:, None] % LEAF
    column_place = jnp.arange(LEAF)[None, :]
    diagonal = jnp.exp(jax.random.uniform(first_key, (POINTS, LEAF), minval=jnp.log(0.5), maxval=jnp.log(2.0)))
    off_diagonal = jax.random.normal(second_key, (POINTS, LEAF)) * (0.5 / LEAF ** 0.5)
    return jnp.where(row_place == column_place, diagonal, off_diagonal).astype(jnp.float32).astype(jnp.bfloat16)


def draw_basis_right(key, part):
    level_ids = jnp.arange(LEVELS)[:, None, None].astype(jnp.float32)
    half_sizes = POINTS / 2.0 / 2.0 ** level_ids
    base = jax.random.normal(key, (LEVELS, POINTS, RANK))
    return (base / jnp.sqrt(half_sizes)).astype(jnp.float32)


def chord_layout(key):
    offset_key = jax.random.fold_in(key, 21)
    level_key = jax.random.fold_in(key, 22)
    forced_key = jax.random.fold_in(key, 23)
    start_key = jax.random.fold_in(key, 24)
    cell_total = 4 * BLK_DEV
    offsets = jax.random.randint(offset_key, (N_PTS,), 0, 4).astype(jnp.int32)
    level_draw = jax.random.randint(level_key, (N_PTS,), 0, 8)
    widths = jnp.where(level_draw < 5, 1, jnp.where(level_draw < 7, 3, 6)).astype(jnp.int32)
    forced = jax.random.randint(forced_key, (), 0, N_PTS)
    widths = jnp.where(jnp.arange(N_PTS) == forced, 6, widths).astype(jnp.int32)
    starts = jax.random.randint(start_key, (N_PTS,), 1, cell_total - 6).astype(jnp.int32)
    return (offsets, widths, starts)


def table_pair(key):
    offsets, widths, starts = chord_layout(key)
    lower = (starts - 1)[:, None] - offsets[None, :]
    upper = (starts + widths)[:, None] - offsets[None, :]
    first_live = jnp.maximum((lower + 3) // 4, 0)
    last_live = jnp.minimum(upper // 4, BLK_DEV - 1)
    live_total = jnp.maximum(last_live - first_live + 1, 0)
    first = jnp.minimum(first_live, BLK_DEV - CAP)
    count = jnp.where(live_total > 0, last_live - first + 1, 0)
    return (first.astype(jnp.int32), count.astype(jnp.int32))


def draw_block_first(key, part):
    return table_pair(key)[0]


def draw_block_count(key, part):
    return table_pair(key)[1]


def draw_point_pos(key, part):
    offsets, widths, starts = chord_layout(key)
    gap_key = jax.random.fold_in(key, 31)
    gaps = jax.random.uniform(gap_key, (N_PTS, BLK_DEV, LEAF), minval=0.2, maxval=1.0)
    running = jnp.cumsum(gaps, axis=2)
    inside = 0.999 * (running - gaps[:, :, :1]) / running[:, :, -1:]
    cells = (offsets[:, None] + 4 * jnp.arange(BLK_DEV)[None, :]).astype(jnp.float32)
    return (cells[:, :, None] + inside).reshape(POINTS).astype(jnp.float32)


def draw_map_pos(key, part):
    offsets, widths, starts = chord_layout(key)
    spot_key = jax.random.fold_in(key, 32)
    spots = jax.random.uniform(spot_key, (N_PTS, MAP_DEV), minval=0.0, maxval=0.999)
    placed = starts.astype(jnp.float32)[:, None] + widths.astype(jnp.float32)[:, None] * spots
    return placed.reshape(MAPS).astype(jnp.float32)


def level_of(own_key, shape, shards, low, largest):
    level, own = 1.0, jax.random.fold_in(own_key, 6)
    for position, parts in shards:
        steps = jnp.exp(jax.random.uniform(jax.random.fold_in(own, position), (parts,), jnp.float32, low / len(shards), largest / len(shards)))
        level = level * jnp.repeat(steps, shape[position] // parts).reshape([-1 if axis == position else 1 for axis in range(len(shape))])
    return level


def noise(rng, shape, spread, reach, pieces=(), kind=jnp.bfloat16):
    entries = jax.random.normal(rng, shape, jnp.float32) * spread
    if len(pieces) > 0:
        entries = level_of(rng, shape, pieces, -0.22, 0.18) * entries
    return jnp.clip(entries, min=-reach, max=reach).astype(kind)


def setup_inputs(seed: int = 0, part: int = 0) -> dict:
    key_of = jax.random.split(jax.random.key(seed), 10)
    part_splits = jax.random.split(jax.random.fold_in(key_of[9], part), 10)
    return {
        "residual_cols": noise(part_splits[0], (POINTS, SAMPLES), 1.0, 6.0, ((0, 32),)),
        "leaf_inverse": draw_leaf_inverse(jax.random.fold_in(jax.random.fold_in(key_of[9], part), 71), part),
        "basis_left": noise(part_splits[2], (LEVELS, POINTS, RANK), (10 * RANK) ** -0.5, 0.15625, ((1, 32),), jnp.float32),
        "basis_right": draw_basis_right(jax.random.fold_in(jax.random.fold_in(key_of[9], part), 71), part),
        "point_pos": draw_point_pos(jax.random.fold_in(key_of[9], 71), part),
        "map_pos": draw_map_pos(jax.random.fold_in(key_of[9], 71), part),
        "prior_map": noise(part_splits[6], (MAPS, SAMPLES), 1.0, 6.0, ((0, 32),)),
        "block_first": draw_block_first(jax.random.fold_in(key_of[9], 71), part),
        "block_count": draw_block_count(jax.random.fold_in(key_of[9], 71), part),
    }


amplitude = 0.2
highest = lax.Precision.HIGHEST


def wendland(distance):
    scaled = jnp.minimum(jnp.abs(distance) * (2.0 * LEAF), 1.0)
    return (1.0 - scaled) ** 4 * (1.0 + 4.0 * scaled)


def reference(residual_cols, leaf_inverse, basis_left, basis_right, point_pos, map_pos, prior_map, block_first, block_count):
    block_total = POINTS // LEAF
    inverses = leaf_inverse.reshape(block_total, LEAF, LEAF).astype(jnp.float32)
    right_side = residual_cols.reshape(block_total, LEAF, SAMPLES).astype(jnp.float32)
    solved = jnp.einsum("bij,bjs->bis", inverses, right_side, precision=highest).reshape(POINTS, SAMPLES)
    for level_index in reversed(range(LEVELS)):
        half_size = POINTS // 2 ** (level_index + 1)
        node_count = POINTS // (2 * half_size)
        coeff_view = solved.reshape(node_count, 2, half_size, SAMPLES)
        right_view = basis_right[level_index].reshape(node_count, 2, half_size, RANK)
        left_view = basis_left[level_index].reshape(node_count, 2, half_size, RANK)
        projected = jnp.einsum("nhpr,nhps->nhrs", right_view, coeff_view, precision=highest)
        sibling = projected[:, ::-1]
        update = jnp.einsum("nhpr,nhrs->nhps", left_view, sibling, precision=highest)
        solved = solved + update.reshape(POINTS, SAMPLES)
    coeffs = solved.astype(jnp.bfloat16)
    coeff_blocks = coeffs.reshape(N_PTS, BLK_DEV, LEAF, SAMPLES)
    position_blocks = point_pos.reshape(N_PTS, BLK_DEV, LEAF)
    sources = jnp.arange(N_PTS, dtype=jnp.int32)[:, None]
    slot_range = jnp.arange(CAP, dtype=jnp.int32)[None, :]

    def owner_map(owner):
        slot_index = block_first[owner][:, None] + slot_range
        live = slot_range < block_count[owner][:, None]
        data = coeff_blocks[sources, slot_index]
        positions = position_blocks[sources, slot_index]
        targets = lax.dynamic_slice_in_dim(map_pos, owner * MAP_DEV, MAP_DEV)
        kernel = amplitude * wendland(targets[:, None, None, None] - positions[None])
        weights = jnp.where(live[None, :, :, None], kernel, 0.0).astype(jnp.bfloat16)
        return jnp.dot(weights.reshape(MAP_DEV, -1), data.reshape(-1, SAMPLES), preferred_element_type=jnp.float32)

    terms = lax.map(owner_map, jnp.arange(N_PTS, dtype=jnp.int32))
    sample_map = prior_map.astype(jnp.float32) + terms.reshape(MAPS, SAMPLES)
    return solved, sample_map
```

```python
import functools

import jax
import jax.numpy as jnp
from jax import lax
from jax.experimental import pallas as pl
from jax.experimental.pallas import tpu as pltpu
from jax.sharding import PartitionSpec as P

AMPLITUDE = 0.2
FAR = -1e6
PIECES = 4
TOGETHER = 4
SPLIT = (1,)
SENDS = 17
f32 = jnp.float32
bf16 = jnp.bfloat16


def mm(a, b):
    return jnp.dot(a, b, preferred_element_type=f32)


def kernel(
    n,
    leaf,
    res_hbm,
    inv_hbm,
    bl_hbm,
    br_hbm,
    pp_hbm,
    mp_hbm,
    prior_hbm,
    first_hbm,
    count_hbm,
    out_hbm,
    map_ref,
    res_ref,
    inv_ref,
    bl_ref,
    br_ref,
    pu,
    mp_ref,
    prior_ref,
    first_ref,
    count_ref,
    xs,
    rth,
    lh,
    gf,
    gs,
    gr,
    tf,
    ts,
    tr,
    cbuf,
    co,
    ps,
    mpb,
    wts,
    acc,
    ms,
    mr,
    fs,
    fr,
    ss,
    sr,
    lt,
    lr,
    zs,
    zr,
    send_sem,
    recv_sem,
    load_sem,
    store_sem,
):
    rows, samples = res_ref.shape
    rank = bl_ref.shape[2]
    levels = bl_ref.shape[0]
    half = samples // 2
    depth = n.bit_length() - 1
    tile = prior_ref.shape[0]
    late = samples // rank
    early = depth - late
    me = lax.axis_index("pts")
    bits = [lax.rem(me // 2**k, 2) for k in range(depth)]
    par = bits[0]
    pool = [None] * send_sem.shape[0]
    arrivals = []
    sends = []

    def partner(mask):
        device = me
        for k in range(depth):
            if (mask >> k) & 1:
                device = device + 2**k * (1 - 2 * bits[k])
        return device

    def describe(src, dst, send, recv, mask):
        return pltpu.make_async_remote_copy(
            src_ref=src,
            dst_ref=dst,
            send_sem=send_sem.at[send],
            recv_sem=recv_sem.at[recv],
            device_id={"pts": partner(mask)},
            device_id_type=pl.DeviceIdType.MESH,
        )

    def arrival():
        arrivals.append(len(arrivals))
        return arrivals[-1]

    def remote(src, dst, mask):
        slot = len(sends) % (len(pool) - 1) + 1
        if pool[slot] is not None:
            pool[slot].wait_send()
        copy = describe(src, dst, slot, arrival(), mask)
        copy.start()
        pool[slot] = copy
        sends.append(copy)
        return copy

    loads = {}

    def load(name, src, dst):
        loads[name] = pltpu.make_async_copy(src, dst, load_sem.at[len(loads)])
        loads[name].start()

    tree = pl.ds(0, depth)
    load("r", br_hbm.at[tree], br_ref.at[tree])
    load("l", bl_hbm.at[tree], bl_ref.at[tree])
    load("inv", inv_hbm, inv_ref)
    load("res", res_hbm, res_ref)
    for l in range(levels - 1, depth - 1, -1):
        load(("r", l), br_hbm.at[l], br_ref.at[l])
        load(("l", l), bl_hbm.at[l], bl_ref.at[l])

    barrier = pltpu.get_barrier_semaphore()
    for mask in range(1, n):
        pl.semaphore_signal(
            barrier, inc=1, device_id={"pts": partner(mask)}, device_id_type=pl.DeviceIdType.MESH
        )
    load("mp", mp_hbm, mp_ref)
    load("pp", pp_hbm.at[me], pu)
    load("first", first_hbm, first_ref)
    load("count", count_hbm, count_ref)
    load("prior", prior_hbm, prior_ref)

    pairs = [m * (m + 1) // 2 for m in range(depth)]
    g_off, t_off = [], []
    g_at = t_at = 0
    for k in range(depth):
        m = depth - 1 - k
        g_off.append(g_at)
        t_off.append(t_at)
        g_at += pairs[m]
        t_at += m + 1

    loads["r"].wait()
    for l in range(depth - 1, -1, -1):
        rth[l * rank : (l + 1) * rank, :] = br_ref[l].astype(bf16).T
    loads["l"].wait()
    for l in range(depth - 1, -1, -1):
        lh[:, l * rank : (l + 1) * rank] = bl_ref[l].astype(bf16)
    for m in range(depth - 1, 0, -2):
        low = max(m - 1, 1)
        product = mm(rth[: m * rank, :], lh[:, low * rank : (m + 1) * rank])
        for i in range(m, low - 1, -1):
            start = sum(range(i + 1, depth))
            part = product[: i * rank, (i - low) * rank : (i - low + 1) * rank]
            part = part.reshape(i, rank, rank)
            gf[start : start + i] = part
            gs[start : start + i] = part.astype(bf16)
    for name in ("mp", "pp", "first", "count", "prior"):
        loads[name].wait()
    mpb[0] = jnp.zeros((1, 128), f32)
    mpb[0, :, :tile] = mp_ref[0]

    with jax.named_scope("barrier"):
        pl.semaphore_wait(barrier, n - 1)

    group = 2**early
    spots = []
    for first_mask in range(0, n, group):
        low = max(first_mask, 1)
        recv = arrival()
        for mask in range(low, first_mask + group):
            describe(mpb.at[0], mpb.at[mask], 0, recv, mask).start()
        view = mpb.at[pl.ds(low, first_mask + group - low)]
        spots.append(describe(view, view, 0, recv, 1))
    others = mpb.at[pl.ds(1, n - 1)]
    pool[0] = describe(others, others, 0, 0, 1)

    g_copies = {}
    rank_half = rank // 2
    core_rows = pl.ds(pl.multiple_of(par * rank_half, rank_half), rank_half)

    def g_span(k, part):
        m = depth - 1 - k
        if part == "head":
            return g_off[k], m
        return g_off[k] + m, pairs[m] - m

    def g_send(k, part):
        start, size = g_span(k, part)
        if size == 0:
            return
        span = pl.ds(start, size)
        if k in SPLIT:
            copy = remote(gs.at[span, core_rows], gr.at[span, core_rows], 2**k)
        else:
            copy = remote(gs.at[span], gr.at[span], 2**k)
        g_copies[k, part] = copy

    def g_relay(k, part):
        start, size = g_span(k, part)
        if k not in SPLIT or size == 0:
            return
        g_copies[k, part].wait_recv()
        view = gr.at[pl.ds(start, size), core_rows]
        g_copies[k, part] = remote(view, view, 1)

    def g_wait(k, part):
        if (k, part) in g_copies:
            g_copies.pop((k, part)).wait_recv()

    def g_next(k):
        start, size = g_span(k, "rest")
        if size == 0:
            return
        g_wait(k, "rest")
        total = gf[start : start + size] + gr[start : start + size].astype(f32)
        gf[g_off[k + 1] : g_off[k + 1] + size] = total
        gs[g_off[k + 1] : g_off[k + 1] + size] = total.astype(bf16)

    g_send(0, "rest")
    g_send(0, "head")

    loads["inv"].wait()
    loads["res"].wait()
    for b in range(rows // leaf):
        view = slice(b * leaf, (b + 1) * leaf)
        xs[view, :] = mm(inv_ref[view, :], res_ref[view, :])
    total_rows = rows * n
    for level in range(levels - 1, depth - 1, -1):
        loads["r", level].wait()
        loads["l", level].wait()
        size = total_rows // 2 ** (level + 1)
        count = rows // size
        projected = []
        for a in range(count):
            view = slice(a * size, (a + 1) * size)
            part = mm(br_ref[level, view, :].astype(bf16).T, xs[view, :].astype(bf16))
            projected.append(part.astype(bf16))
        for a in range(count):
            view = slice(a * size, (a + 1) * size)
            xs[view, :] += mm(bl_ref[level, view, :].astype(bf16), projected[a ^ 1])
    t_all = mm(rth[...], xs[...].astype(bf16))
    for h in range(2):
        t_half = t_all[:, h * half : (h + 1) * half].reshape(depth, rank, half)
        tf[h] = t_half
        ts[h, pl.ds(0, depth)] = t_half.astype(bf16)

    top = depth - 1
    t_copies = {
        (0, "urgent"): [
            remote(ts.at[1 - par, pl.ds(late, depth - late)], tr.at[pl.ds(late, depth - late)], 1),
            remote(ts.at[par, top], cbuf.at[top, par], 1),
        ],
        (0, "rest"): [remote(ts.at[1 - par, pl.ds(0, late)], tr.at[pl.ds(0, late)], 1)],
    }

    def combine(k, low, high):
        m = depth - 1 - k
        if high <= low:
            return
        count = high - low
        mine = ts[par, t_off[k] + m]
        theirs = tr[t_off[k] + m]
        g_mine = gs[g_off[k] + low : g_off[k] + high].reshape(count * rank, rank)
        g_theirs = gr[g_off[k] + low : g_off[k] + high].reshape(count * rank, rank)
        gained = mm(g_mine, theirs) + mm(g_theirs, mine)
        total = (
            tf[par, low:high]
            + tr[t_off[k] + low : t_off[k] + high].astype(f32)
            + gained.reshape(count, rank, half)
        )
        tf[par, low:high] = total
        ts[par, t_off[k + 1] + low : t_off[k + 1] + high] = total.astype(bf16)

    def t_send(k, low, high, name):
        span = pl.ds(t_off[k] + low, high - low)
        t_copies[k, name] = [remote(ts.at[par, span], tr.at[span], 2**k)]

    def t_wait(k, name):
        for copy in t_copies.pop((k, name), []):
            copy.wait_recv()

    forwards = {}

    def forward(k):
        m = depth - 1 - k
        forwards[m] = remote(tr.at[t_off[k] + m], cbuf.at[m, par], 1)

    def weights(low_e, high_e):
        with jax.named_scope(f"spot{low_e}"):
            spots[low_e // group].wait_recv()
        own_u = pu[...]

        def one(e):
            spot = 0
            other = 0
            for i in range(depth):
                bit = lax.rem(e // 2**i, 2)
                spot = spot + bit * 2 ** (depth - 1 - i)
                other = other + lax.rem(bit + bits[i], 2) * 2**i
            first = first_ref[other, me]
            last = first + count_ref[other, me]
            t_col = jnp.broadcast_to(mpb[e], (128, 128)).T[:tile]
            base = pl.multiple_of(spot * tile, tile)
            for b in range(rows // leaf):
                u_row = own_u[:, b * leaf : (b + 1) * leaf]
                listed = jnp.logical_and(first <= b, b < last)
                u_row = jnp.where(listed, u_row, FAR)
                scaled = jnp.minimum(jnp.abs(t_col - u_row) * (2.0 * leaf), 1.0)
                rest = 1.0 - scaled
                square = rest * rest
                value = AMPLITUDE * (square * square * (1.0 + 4.0 * scaled))
                wts[pl.ds(base, tile), b * leaf : (b + 1) * leaf] = value.astype(bf16)

        def several(i, carry):
            for j in range(TOGETHER):
                one(low_e + i * TOGETHER + j)
            return carry

        lax.fori_loop(0, (high_e - low_e) // TOGETHER, several, 0)

    quarter = n // 8 * tile
    half_rows = 4 * quarter
    sums = {}

    def map_first(s, factor, order):
        for j in order:
            low = half_rows + j * quarter
            ms[s, j] = mm(wts[low : low + quarter, :], factor[...]).astype(bf16)
            sums[s, j] = remote(ms.at[s, j], mr.at[s, j], 1)

    def keep(s, j, factor):
        part = mm(wts[j * quarter : (j + 1) * quarter, :], factor[...])
        with jax.named_scope(f"first{s}{j}"):
            sums[s, j].wait_recv()
        part = part + mr[s, j].astype(f32)
        return [part[:, c * half : (c + 1) * half] for c in range(2)]

    def map_second(s, factor):
        def to_x(slot, value):
            fs[s, 0, slot] = value.astype(bf16)
            sums[s, "x", slot] = remote(fs.at[s, 0, slot], fr.at[s, 0, slot], 2)

        def to_y(slot, value):
            fs[s, 1, slot] = value.astype(bf16)
            sums[s, "y", slot] = remote(fs.at[s, 1, slot], fr.at[s, 1, slot], 4)

        part = keep(s, 3, factor)
        to_x(1, part[0])
        to_y(1, part[1])
        part = keep(s, 2, factor)
        to_x(0, part[0])
        acc[s, 1, 1] = part[1]
        part = keep(s, 1, factor)
        to_y(0, part[1])
        acc[s, 0, 1] = part[0]
        part = keep(s, 0, factor)
        acc[s, 0, 0] = part[0]
        acc[s, 1, 0] = part[1]

    def map_third(s):
        with jax.named_scope(f"third{s}"):
            sums[s, "x", 1].wait_recv()
        ss[s, 0] = (acc[s, 0, 1] + fr[s, 0, 1].astype(f32)).astype(bf16)
        sums[s, "xy"] = remote(ss.at[s, 0], sr.at[s, 0], 4)
        with jax.named_scope(f"thirdb{s}"):
            sums[s, "y", 1].wait_recv()
        ss[s, 1] = (acc[s, 1, 1] + fr[s, 1, 1].astype(f32)).astype(bf16)
        sums[s, "yx"] = remote(ss.at[s, 1], sr.at[s, 1], 2)

    def map_fourth(s):
        with jax.named_scope(f"fourth{s}"):
            for name in ((s, "x", 0), (s, "y", 0), (s, "xy"), (s, "yx")):
                sums[name].wait_recv()
        size = quarter
        for c in range(2):
            acc[s, c, 0] += fr[s, c, 0].astype(f32) + sr[s, c].astype(f32)
        base = 0
        for k in range(3, early):
            size = size // 2
            for c in range(2):
                lt[s, c, base : base + size, :] = acc[s, c, 0, size : 2 * size, :].astype(bf16)
            view = pl.ds(base, size)
            copy = remote(lt.at[s, :, view], lr.at[s, :, view], 2**k)
            copy.wait_recv()
            for c in range(2):
                acc[s, c, 0, :size, :] += lr[s, c, base : base + size, :].astype(f32)
            base += size
        return jnp.concatenate([acc[s, c, 0, :size, :] for c in range(2)], axis=1)

    late_factor = lh.at[:, pl.ds(0, late * rank)]

    def urgent(k):
        m = depth - 1 - k
        with jax.named_scope(f"turgent{k}"):
            t_wait(k, "urgent")
        if k > 0:
            forward(k)
        if m > late:
            with jax.named_scope(f"ghead{k}"):
                g_wait(k, "head")
            combine(k, late, m)
            t_send(k + 1, late, m, "urgent")

    def rest(k):
        with jax.named_scope(f"trest{k}"):
            t_wait(k, "rest")
        with jax.named_scope(f"gheadb{k}"):
            g_wait(k, "head")
        combine(k, 0, min(late, depth - 1 - k))
        t_send(k + 1, 0, min(late, depth - 1 - k), "rest")

    def factors(k):
        with jax.named_scope(f"gnext{k}"):
            g_next(k)
        g_send(k + 1, "head")
        g_send(k + 1, "rest")

    with jax.named_scope("gnext0"):
        g_next(0)
    g_send(1, "head")
    urgent(0)
    g_send(1, "rest")
    rest(0)
    for i in range(n // group):
        weights(i * group, (i + 1) * group)
        if i == 1:
            with jax.named_scope("relay0"):
                g_relay(1, "head")
    for k in range(1, early):
        if k > 1 and depth - 1 - k > late:
            factors(k - 1)
        urgent(k)
        if k == 1:
            map_first(0, late_factor, (3, 2))
            with jax.named_scope("relay1"):
                g_relay(1, "rest")
            map_first(0, late_factor, (1, 0))
        else:
            if depth - 1 - k <= late:
                factors(k - 1)
            rest(k - 1)
    map_second(0, late_factor)

    mine_cols = pl.ds(pl.multiple_of(par * half, half), half)
    other_cols = pl.ds(pl.multiple_of((1 - par) * half, half), half)

    def own(m):
        return tr[t_off[depth - 1 - m] + m]

    def sibling(m):
        return cbuf[m, 1 - par]

    def finish(columns, parts):
        stacked = jnp.concatenate(parts, axis=0)
        ps[late * rank :, columns] = stacked
        co[:, columns] = (xs[:, columns] + mm(lh[:, late * rank :], stacked)).astype(bf16)

    finish(mine_cols, [own(m) for m in range(late, depth)])
    with jax.named_scope("forwards"):
        for m in range(late, depth - 1):
            forwards[m].wait_recv()
    finish(other_cols, [sibling(m) for m in range(late, depth)])
    map_first(1, co, (3, 2, 1, 0))
    rest(early - 1)
    factors(early - 1)
    map_third(0)
    map_second(1, co)
    for k in range(early, depth):
        with jax.named_scope(f"turgent{k}"):
            t_wait(k, "rest")
        forward(k)
        if k < depth - 1:
            rest(k)
            factors(k)
        if k == early:
            map_third(1)
            corrections = map_fourth(0).astype(bf16)
            partial = map_fourth(1)
    for m in range(late):
        ps[m * rank : (m + 1) * rank, mine_cols] = own(m)
    with jax.named_scope("forwards2"):
        for m in range(late):
            forwards[m].wait_recv()
    for m in range(late):
        ps[m * rank : (m + 1) * rank, other_cols] = sibling(m)
    total = partial + mm(corrections, ps[: late * rank])
    lines = []
    for v in (3, 1, 2):
        mask = 0
        for i in range(late):
            mask += ((v >> (late - 1 - i)) & 1) * 2 ** (early + i)
        zs[v] = total[v * tile : (v + 1) * tile].astype(bf16)
        lines.append((v, remote(zs.at[v], zr.at[v], mask)))
    xs[...] += mm(lh[...], ps[...])
    for l in range(depth):
        view = slice(l * rank, (l + 1) * rank)
        low = (bl_ref[l] - lh[:, view].astype(f32)).astype(bf16)
        xs[...] += mm(low, ps[view, :])
    store = pltpu.make_async_copy(xs, out_hbm, store_sem.at[0])
    store.start()
    result = prior_ref[...].astype(f32) + total[:tile]
    for v, copy in lines:
        with jax.named_scope(f"line{v}"):
            copy.wait_recv()
        result = result + zr[v].astype(f32)
    map_ref[...] = result
    with jax.named_scope("end"):
        store.wait()
        for copy in pool:
            copy.wait_send()
    assert len(arrivals) == recv_sem.shape[0], len(arrivals)


def deliver(solved_ref, mapped_ref, out_ref, map_ref, held, spots, in_sem, out_sem):
    piece = held.shape[0] // PIECES
    moves = [(mapped_ref, spots, map_ref)]
    for i in range(PIECES):
        view = pl.ds(i * piece, piece)
        moves.append((solved_ref.at[view], held.at[view], out_ref.at[view]))
    reads = [pltpu.make_async_copy(a, b, in_sem.at[i]) for i, (a, b, _) in enumerate(moves)]
    writes = [pltpu.make_async_copy(b, c, out_sem.at[i]) for i, (_, b, c) in enumerate(moves)]
    for read in reads:
        read.start()
    for read, write in zip(reads, writes):
        read.wait()
        write.start()
    for write in writes:
        write.wait()


def body(
    residual_cols,
    leaf_inverse,
    basis_left,
    basis_right,
    point_pos,
    map_pos,
    prior_map,
    block_first,
    block_count,
):
    rows, samples = residual_cols.shape
    leaf = leaf_inverse.shape[1]
    levels, _, rank = basis_left.shape
    n = lax.axis_size("pts")
    depth = n.bit_length() - 1
    tile = map_pos.shape[0]
    half = samples // 2
    late = samples // rank
    pair_total = sum(m * (m + 1) // 2 for m in range(depth))
    t_total = depth * (depth + 1) // 2
    vmem = pl.BlockSpec(memory_space=pltpu.VMEM)
    anywhere = pl.BlockSpec(memory_space=pl.ANY)
    line = 2**late
    early = depth - late
    products = sum((2 if m > 1 else 1) * (2 if depth - 1 - m in SPLIT else 1) for m in range(1, depth))
    copies = line + 2 * early + late + depth + products + 2 * (early + 7) + line - 1
    quarter = n // 8 * tile
    solved, mapped = pl.pallas_call(
        functools.partial(kernel, n, leaf),
        out_shape=(
            jax.ShapeDtypeStruct((rows, samples), f32),
            jax.ShapeDtypeStruct((tile, samples), f32),
        ),
        in_specs=[anywhere] * 9,
        out_specs=(anywhere, vmem),
        scratch_shapes=[
            pltpu.VMEM((rows, samples), bf16),
            pltpu.VMEM((rows, leaf), bf16),
            pltpu.VMEM((levels, rows, rank), f32),
            pltpu.VMEM((levels, rows, rank), f32),
            pltpu.VMEM((1, rows), f32),
            pltpu.VMEM((1, 1, tile), f32),
            pltpu.VMEM((tile, samples), bf16),
            pltpu.SMEM((n, n), jnp.int32),
            pltpu.SMEM((n, n), jnp.int32),
            pltpu.VMEM((rows, samples), f32),
            pltpu.VMEM((depth * rank, rows), bf16),
            pltpu.VMEM((rows, depth * rank), bf16),
            pltpu.VMEM((pair_total, rank, rank), f32),
            pltpu.VMEM((pair_total, rank, rank), bf16),
            pltpu.VMEM((pair_total, rank, rank), bf16),
            pltpu.VMEM((2, depth, rank, half), f32),
            pltpu.VMEM((2, t_total, rank, half), bf16),
            pltpu.VMEM((t_total, rank, half), bf16),
            pltpu.VMEM((depth, 2, rank, half), bf16),
            pltpu.VMEM((rows, samples), bf16),
            pltpu.VMEM((depth * rank, samples), bf16),
            pltpu.VMEM((n, 1, 128), f32),
            pltpu.VMEM((n * tile, rows), bf16),
            pltpu.VMEM((2, 2, 2, quarter, half), f32),
            pltpu.VMEM((2, 4, quarter, samples), bf16),
            pltpu.VMEM((2, 4, quarter, samples), bf16),
            pltpu.VMEM((2, 2, 2, quarter, half), bf16),
            pltpu.VMEM((2, 2, 2, quarter, half), bf16),
            pltpu.VMEM((2, 2, quarter, half), bf16),
            pltpu.VMEM((2, 2, quarter, half), bf16),
            pltpu.VMEM((2, 2, quarter, half), bf16),
            pltpu.VMEM((2, 2, quarter, half), bf16),
            pltpu.VMEM((line, tile, samples), bf16),
            pltpu.VMEM((line, tile, samples), bf16),
            pltpu.SemaphoreType.DMA((SENDS,)),
            pltpu.SemaphoreType.DMA((copies,)),
            pltpu.SemaphoreType.DMA((2 * (levels - depth) + 9,)),
            pltpu.SemaphoreType.DMA((1,)),
        ],
        compiler_params=pltpu.CompilerParams(
            collective_id=0, has_side_effects=True, vmem_limit_bytes=60 * 1024 * 1024
        ),
    )(
        residual_cols,
        leaf_inverse,
        basis_left,
        basis_right,
        point_pos.reshape(n, 1, rows),
        map_pos.reshape(1, 1, tile),
        prior_map,
        block_first,
        block_count,
    )
    return pl.pallas_call(
        deliver,
        out_shape=(
            jax.ShapeDtypeStruct((rows, samples), f32),
            jax.ShapeDtypeStruct((tile, samples), f32),
        ),
        in_specs=[anywhere] * 2,
        out_specs=(anywhere, anywhere),
        scratch_shapes=[
            pltpu.VMEM((rows, samples), f32),
            pltpu.VMEM((tile, samples), f32),
            pltpu.SemaphoreType.DMA((PIECES + 1,)),
            pltpu.SemaphoreType.DMA((PIECES + 1,)),
        ],
    )(solved, mapped)


def solution(mesh):
    in_specs = (
        P(("groups", "pts"), None),
        P(("groups", "pts"), None),
        P(None, ("groups", "pts"), None),
        P(None, ("groups", "pts"), None),
        P(),
        P("pts"),
        P(("groups", "pts"), None),
        P(),
        P(),
    )
    out_specs = (P(("groups", "pts"), None), P(("groups", "pts"), None))
    return jax.shard_map(body, mesh=mesh, in_specs=in_specs, out_specs=out_specs, check_vma=False)
```

```python
import functools

import jax
import jax.numpy as jnp
from jax import lax
from jax.experimental import pallas as pl
from jax.experimental.pallas import tpu as pltpu
from jax.sharding import PartitionSpec as P

AMPLITUDE = 0.2
FAR = -1e6
PIECES = 4
TOGETHER = 4
SPLIT = (1,)
SENDS = 17
VMEM_LIMIT = 50 * 1024 * 1024
f32 = jnp.float32
bf16 = jnp.bfloat16


def mm(a, b):
    return jnp.dot(a, b, preferred_element_type=f32)


def kernel(
    n,
    leaf,
    res_hbm,
    inv_hbm,
    bl_hbm,
    br_hbm,
    pp_hbm,
    mp_hbm,
    prior_hbm,
    first_hbm,
    count_hbm,
    xs,
    map_ref,
    res_ref,
    inv_ref,
    bl_ref,
    br_ref,
    pu,
    mp_ref,
    prior_ref,
    first_ref,
    count_ref,
    rth,
    lh,
    gf,
    gs,
    gr,
    tf,
    ts,
    tr,
    cbuf,
    co,
    ps,
    mpb,
    wts,
    acc,
    ms,
    mr,
    fs,
    fr,
    ss,
    sr,
    lt,
    lr,
    zs,
    zr,
    send_sem,
    recv_sem,
    load_sem,
):
    rows, samples = res_ref.shape
    rank = bl_ref.shape[2]
    levels = bl_ref.shape[0]
    half = samples // 2
    depth = n.bit_length() - 1
    tile = prior_ref.shape[0]
    late = samples // rank
    early = depth - late
    me = lax.axis_index("pts")
    bits = [lax.rem(me // 2**k, 2) for k in range(depth)]
    par = bits[0]
    pool = [None] * send_sem.shape[0]
    arrivals = []
    sends = []

    def partner(mask):
        device = me
        for k in range(depth):
            if (mask >> k) & 1:
                device = device + 2**k * (1 - 2 * bits[k])
        return device

    def describe(src, dst, send, recv, mask):
        return pltpu.make_async_remote_copy(
            src_ref=src,
            dst_ref=dst,
            send_sem=send_sem.at[send],
            recv_sem=recv_sem.at[recv],
            device_id={"pts": partner(mask)},
            device_id_type=pl.DeviceIdType.MESH,
        )

    def arrival():
        arrivals.append(len(arrivals))
        return arrivals[-1]

    def remote(src, dst, mask):
        slot = len(sends) % (len(pool) - 1) + 1
        if pool[slot] is not None:
            pool[slot].wait_send()
        copy = describe(src, dst, slot, arrival(), mask)
        copy.start()
        pool[slot] = copy
        sends.append(copy)
        return copy

    loads = {}

    def load(name, src, dst):
        loads[name] = pltpu.make_async_copy(src, dst, load_sem.at[len(loads)])
        loads[name].start()

    load("inv", inv_hbm, inv_ref)
    load("res", res_hbm, res_ref)
    tree = pl.ds(0, depth)
    load("r", br_hbm.at[tree], br_ref.at[tree])
    load("l", bl_hbm.at[tree], bl_ref.at[tree])
    for l in range(levels - 1, depth - 1, -1):
        load(("r", l), br_hbm.at[l], br_ref.at[l])
        load(("l", l), bl_hbm.at[l], bl_ref.at[l])

    barrier = pltpu.get_barrier_semaphore()
    for mask in range(1, n):
        pl.semaphore_signal(
            barrier, inc=1, device_id={"pts": partner(mask)}, device_id_type=pl.DeviceIdType.MESH
        )
    load("mp", mp_hbm, mp_ref)
    load("pp", pp_hbm.at[me], pu)
    load("first", first_hbm, first_ref)
    load("count", count_hbm, count_ref)
    load("prior", prior_hbm, prior_ref)

    pairs = [m * (m + 1) // 2 for m in range(depth)]
    g_off, t_off = [], []
    g_at = t_at = 0
    for k in range(depth):
        m = depth - 1 - k
        g_off.append(g_at)
        t_off.append(t_at)
        g_at += pairs[m]
        t_at += m + 1

    loads["inv"].wait()
    loads["res"].wait()
    for b in range(rows // leaf):
        view = slice(b * leaf, (b + 1) * leaf)
        xs[view, :] = mm(inv_ref[view, :], res_ref[view, :])
    loads["r"].wait()
    for l in range(depth - 1, -1, -1):
        rth[l * rank : (l + 1) * rank, :] = br_ref[l].astype(bf16).T
    loads["l"].wait()
    for l in range(depth - 1, -1, -1):
        lh[:, l * rank : (l + 1) * rank] = bl_ref[l].astype(bf16)
    for m in range(depth - 1, 0, -2):
        low = max(m - 1, 1)
        product = mm(rth[: m * rank, :], lh[:, low * rank : (m + 1) * rank])
        for i in range(m, low - 1, -1):
            start = sum(range(i + 1, depth))
            part = product[: i * rank, (i - low) * rank : (i - low + 1) * rank]
            part = part.reshape(i, rank, rank)
            gf[start : start + i] = part
            gs[start : start + i] = part.astype(bf16)
    for name in ("mp", "pp", "first", "count", "prior"):
        loads[name].wait()
    mpb[0] = jnp.zeros((1, 128), f32)
    mpb[0, :, :tile] = mp_ref[0]

    with jax.named_scope("barrier"):
        pl.semaphore_wait(barrier, n - 1)

    group = 2**early
    spots = []
    for first_mask in range(0, n, group):
        low = max(first_mask, 1)
        recv = arrival()
        for mask in range(low, first_mask + group):
            describe(mpb.at[0], mpb.at[mask], 0, recv, mask).start()
        view = mpb.at[pl.ds(low, first_mask + group - low)]
        spots.append(describe(view, view, 0, recv, 1))
    others = mpb.at[pl.ds(1, n - 1)]
    pool[0] = describe(others, others, 0, 0, 1)

    g_copies = {}
    relayed = set()
    rank_half = rank // 2
    core_rows = pl.ds(pl.multiple_of(par * rank_half, rank_half), rank_half)

    def g_span(k, part):
        m = depth - 1 - k
        if part == "head":
            return g_off[k], m
        return g_off[k] + m, pairs[m] - m

    def g_send(k, part):
        start, size = g_span(k, part)
        if size == 0:
            return
        span = pl.ds(start, size)
        if k in SPLIT:
            copy = remote(gs.at[span, core_rows], gr.at[span, core_rows], 2**k)
        else:
            copy = remote(gs.at[span], gr.at[span], 2**k)
        g_copies[k, part] = copy

    def g_relay(k, part):
        start, size = g_span(k, part)
        if k not in SPLIT or size == 0 or (k, part) in relayed:
            return
        relayed.add((k, part))
        g_copies[k, part].wait_recv()
        view = gr.at[pl.ds(start, size), core_rows]
        g_copies[k, part] = remote(view, view, 1)

    def g_wait(k, part):
        if (k, part) in g_copies:
            g_relay(k, part)
            g_copies.pop((k, part)).wait_recv()

    def g_next(k):
        start, size = g_span(k, "rest")
        if size == 0:
            return
        g_wait(k, "rest")
        total = gf[start : start + size] + gr[start : start + size].astype(f32)
        gf[g_off[k + 1] : g_off[k + 1] + size] = total
        gs[g_off[k + 1] : g_off[k + 1] + size] = total.astype(bf16)

    g_send(0, "rest")
    g_send(0, "head")

    total_rows = rows * n
    for level in range(levels - 1, depth - 1, -1):
        loads["r", level].wait()
        loads["l", level].wait()
        size = total_rows // 2 ** (level + 1)
        count = rows // size
        projected = []
        for a in range(count):
            view = slice(a * size, (a + 1) * size)
            part = mm(br_ref[level, view, :].astype(bf16).T, xs[view, :].astype(bf16))
            projected.append(part.astype(bf16))
        for a in range(count):
            view = slice(a * size, (a + 1) * size)
            xs[view, :] += mm(bl_ref[level, view, :].astype(bf16), projected[a ^ 1])
    t_all = mm(rth[...], xs[...].astype(bf16))
    for h in range(2):
        t_half = t_all[:, h * half : (h + 1) * half].reshape(depth, rank, half)
        tf[h] = t_half
        ts[h, pl.ds(0, depth)] = t_half.astype(bf16)

    top = depth - 1
    t_copies = {
        (0, "urgent"): [
            remote(ts.at[1 - par, pl.ds(late, depth - late)], tr.at[pl.ds(late, depth - late)], 1),
            remote(ts.at[par, top], cbuf.at[top, par], 1),
        ],
        (0, "rest"): [remote(ts.at[1 - par, pl.ds(0, late)], tr.at[pl.ds(0, late)], 1)],
    }

    def combine(k, low, high):
        m = depth - 1 - k
        if high <= low:
            return
        count = high - low
        mine = ts[par, t_off[k] + m]
        theirs = tr[t_off[k] + m]
        g_mine = gs[g_off[k] + low : g_off[k] + high].reshape(count * rank, rank)
        g_theirs = gr[g_off[k] + low : g_off[k] + high].reshape(count * rank, rank)
        gained = mm(g_mine, theirs) + mm(g_theirs, mine)
        total = (
            tf[par, low:high]
            + tr[t_off[k] + low : t_off[k] + high].astype(f32)
            + gained.reshape(count, rank, half)
        )
        tf[par, low:high] = total
        ts[par, t_off[k + 1] + low : t_off[k + 1] + high] = total.astype(bf16)

    def t_send(k, low, high, name):
        span = pl.ds(t_off[k] + low, high - low)
        t_copies[k, name] = [remote(ts.at[par, span], tr.at[span], 2**k)]

    def t_wait(k, name):
        for copy in t_copies.pop((k, name), []):
            copy.wait_recv()

    forwards = {}

    def forward(k):
        m = depth - 1 - k
        forwards[m] = remote(tr.at[t_off[k] + m], cbuf.at[m, par], 1)

    def weights(place, core):
        if core == 1:
            with jax.named_scope(f"spot{place}"):
                spots[place].wait_recv()
        start = place * group + core
        own_u = pu[...]

        def one(e):
            spot = 0
            other = 0
            for i in range(depth):
                bit = lax.rem(e // 2**i, 2)
                spot = spot + bit * 2 ** (depth - 1 - i)
                other = other + lax.rem(bit + bits[i], 2) * 2**i
            first = first_ref[other, me]
            last = first + count_ref[other, me]
            t_col = jnp.broadcast_to(mpb[e], (128, 128)).T[:tile]
            base = pl.multiple_of(spot * tile, tile)
            for b in range(rows // leaf):
                u_row = own_u[:, b * leaf : (b + 1) * leaf]
                listed = jnp.logical_and(first <= b, b < last)
                u_row = jnp.where(listed, u_row, FAR)
                scaled = jnp.minimum(jnp.abs(t_col - u_row) * (2.0 * leaf), 1.0)
                rest = 1.0 - scaled
                square = rest * rest
                value = AMPLITUDE * (square * square * (1.0 + 4.0 * scaled))
                wts[pl.ds(base, tile), b * leaf : (b + 1) * leaf] = value.astype(bf16)

        def several(i, carry):
            for j in range(TOGETHER):
                one(start + 2 * (i * TOGETHER + j))
            return carry

        lax.fori_loop(0, group // 2 // TOGETHER, several, 0)

    quarter = n // 8 * tile
    half_rows = 4 * quarter
    sums = {}

    def map_first(s, factor, order):
        for j in order:
            low = half_rows + j * quarter
            ms[s, j] = mm(wts[low : low + quarter, :], factor[...]).astype(bf16)
            sums[s, j] = remote(ms.at[s, j], mr.at[s, j], 1)

    def keep(s, j, factor):
        part = mm(wts[j * quarter : (j + 1) * quarter, :], factor[...])
        with jax.named_scope(f"first{s}{j}"):
            sums[s, j].wait_recv()
        part = part + mr[s, j].astype(f32)
        return [part[:, c * half : (c + 1) * half] for c in range(2)]

    def late_second(order):
        for j in order:
            part = keep(0, j, late_factor)
            for c in range(2):
                if j > 1:
                    fs[0, j - 2, c] = part[c].astype(bf16)
                else:
                    acc[0, j, c] = part[c]
            if j == 3:
                sums[0, "x", 1] = remote(fs.at[0, 1], fr.at[0, 1], 2)
            if j == 2:
                sums[0, "x", 0] = remote(fs.at[0, 0, 0], fr.at[0, 0, 0], 2)

    def late_rest():
        sums[0, "x", 2] = remote(fs.at[0, 0, 1], fr.at[0, 0, 1], 2)

    def late_third():
        with jax.named_scope("third0"):
            sums[0, "x", 1].wait_recv()
        ss[0] = (acc[0, 1] + fr[0, 1].astype(f32)).astype(bf16)
        sums[0, "y"] = remote(ss.at[0], sr.at[0], 4)

    def map_second(order):
        def to_x(slot, value):
            fs[1, slot, 0] = value.astype(bf16)
            sums[1, "x", slot] = remote(fs.at[1, slot, 0], fr.at[1, slot, 0], 2)

        def to_y(slot, value):
            fs[1, slot, 1] = value.astype(bf16)
            sums[1, "y", slot] = remote(fs.at[1, slot, 1], fr.at[1, slot, 1], 4)

        for j in order:
            part = keep(1, j, co)
            if j == 3:
                to_x(1, part[0])
                to_y(1, part[1])
            if j == 2:
                to_x(0, part[0])
                acc[1, 1, 1] = part[1]
            if j == 1:
                to_y(0, part[1])
                acc[1, 1, 0] = part[0]
            if j == 0:
                for c in range(2):
                    acc[1, 0, c] = part[c]

    def map_third():
        with jax.named_scope("third1"):
            sums[1, "x", 1].wait_recv()
        ss[1, 0] = (acc[1, 1, 0] + fr[1, 1, 0].astype(f32)).astype(bf16)
        sums[1, "xy"] = remote(ss.at[1, 0], sr.at[1, 0], 4)
        with jax.named_scope("thirdb1"):
            sums[1, "y", 1].wait_recv()
        ss[1, 1] = (acc[1, 1, 1] + fr[1, 1, 1].astype(f32)).astype(bf16)
        sums[1, "yx"] = remote(ss.at[1, 1], sr.at[1, 1], 2)

    def map_fourth(s):
        with jax.named_scope(f"fourth{s}"):
            for name in (("x", 0), ("x", 2), ("y", 0), ("y",), ("xy",), ("yx",)):
                if (s, *name) in sums:
                    sums[(s, *name)].wait_recv()
        size = quarter
        for c in range(2):
            acc[s, 0, c] += fr[s, 0, c].astype(f32) + sr[s, c].astype(f32)
        base = 0
        for k in range(3, early):
            size = size // 2
            for c in range(2):
                lt[s, c, base : base + size, :] = acc[s, 0, c, size : 2 * size, :].astype(bf16)
            view = pl.ds(base, size)
            copy = remote(lt.at[s, :, view], lr.at[s, :, view], 2**k)
            copy.wait_recv()
            for c in range(2):
                acc[s, 0, c, :size, :] += lr[s, c, base : base + size, :].astype(f32)
            base += size
        return jnp.concatenate([acc[s, 0, c, :size, :] for c in range(2)], axis=1)

    late_factor = lh.at[:, pl.ds(0, late * rank)]

    def urgent(k):
        m = depth - 1 - k
        with jax.named_scope(f"turgent{k}"):
            t_wait(k, "urgent")
        if k > 0:
            forward(k)
        if m > late:
            with jax.named_scope(f"ghead{k}"):
                g_wait(k, "head")
            combine(k, late, m)
            t_send(k + 1, late, m, "urgent")

    def rest(k):
        with jax.named_scope(f"trest{k}"):
            t_wait(k, "rest")
        with jax.named_scope(f"gheadb{k}"):
            g_wait(k, "head")
        combine(k, 0, min(late, depth - 1 - k))
        t_send(k + 1, 0, min(late, depth - 1 - k), "rest")

    def factors(k):
        with jax.named_scope(f"gnext{k}"):
            g_next(k)
        g_send(k + 1, "head")
        g_send(k + 1, "rest")

    with jax.named_scope("gnext0"):
        g_next(0)
    g_send(1, "head")
    urgent(0)
    g_send(1, "rest")
    rest(0)
    places = n // group
    for place in range(places):
        weights(place, 1)
    map_first(0, late_factor, (3, 2))
    with jax.named_scope("relay0"):
        g_relay(1, "head")
    map_first(0, late_factor, (1, 0))
    for place in range(places // 2):
        weights(place, 0)
    for k in range(1, early):
        urgent(k)
        if k == 1:
            with jax.named_scope("relay1"):
                g_relay(1, "rest")
            for place in range(places // 2, places):
                weights(place, 0)
            late_second((3, 2))
        if k < early - 1:
            rest(k)
            factors(k)
    late_second((1, 0))

    mine_cols = pl.ds(pl.multiple_of(par * half, half), half)
    other_cols = pl.ds(pl.multiple_of((1 - par) * half, half), half)

    def own(m):
        return tr[t_off[depth - 1 - m] + m]

    def sibling(m):
        return cbuf[m, 1 - par]

    def finish(columns, parts):
        stacked = jnp.concatenate(parts, axis=0)
        ps[late * rank :, columns] = stacked
        co[:, columns] = (xs[:, columns] + mm(lh[:, late * rank :], stacked)).astype(bf16)

    finish(mine_cols, [own(m) for m in range(late, depth)])
    with jax.named_scope("forwards"):
        for m in range(late, depth - 1):
            forwards[m].wait_recv()
    finish(other_cols, [sibling(m) for m in range(late, depth)])
    map_first(1, co, (3, 2, 1, 0))
    map_second((3, 2))
    rest(early - 1)
    factors(early - 1)
    map_second((1, 0))
    late_third()
    for k in range(early, depth):
        with jax.named_scope(f"turgent{k}"):
            t_wait(k, "rest")
        forward(k)
        if k < depth - 1:
            rest(k)
            factors(k)
        if k == early:
            map_third()
            late_rest()
    corrections = map_fourth(0).astype(bf16)
    partial = map_fourth(1)
    for m in range(late):
        ps[m * rank : (m + 1) * rank, mine_cols] = own(m)
    with jax.named_scope("forwards2"):
        for m in range(late):
            forwards[m].wait_recv()
    for m in range(late):
        ps[m * rank : (m + 1) * rank, other_cols] = sibling(m)
    total = partial + mm(corrections, ps[: late * rank])
    lines = []
    for v in (3, 1, 2):
        mask = 0
        for i in range(late):
            mask += ((v >> (late - 1 - i)) & 1) * 2 ** (early + i)
        zs[v] = total[v * tile : (v + 1) * tile].astype(bf16)
        lines.append((v, remote(zs.at[v], zr.at[v], mask)))
    xs[...] += mm(lh[...], ps[...])
    for l in range(depth):
        view = slice(l * rank, (l + 1) * rank)
        low = (bl_ref[l] - lh[:, view].astype(f32)).astype(bf16)
        xs[...] += mm(low, ps[view, :])
    result = prior_ref[...].astype(f32) + total[:tile]
    for v, copy in lines:
        with jax.named_scope(f"line{v}"):
            copy.wait_recv()
        result = result + zr[v].astype(f32)
    map_ref[...] = result
    with jax.named_scope("end"):
        for copy in pool:
            copy.wait_send()
    assert len(arrivals) == recv_sem.shape[0], len(arrivals)


def deliver(solved_ref, mapped_ref, out_ref, map_ref, sems):
    piece = solved_ref.shape[0] // PIECES
    copies = [pltpu.make_async_copy(mapped_ref, map_ref, sems.at[PIECES])]
    for i in range(PIECES):
        view = pl.ds(i * piece, piece)
        copies.append(pltpu.make_async_copy(solved_ref.at[view], out_ref.at[view], sems.at[i]))
    for copy in copies:
        copy.start()
    for copy in copies:
        copy.wait()


def body(
    residual_cols,
    leaf_inverse,
    basis_left,
    basis_right,
    point_pos,
    map_pos,
    prior_map,
    block_first,
    block_count,
):
    rows, samples = residual_cols.shape
    leaf = leaf_inverse.shape[1]
    levels, _, rank = basis_left.shape
    n = lax.axis_size("pts")
    depth = n.bit_length() - 1
    tile = map_pos.shape[0]
    half = samples // 2
    late = samples // rank
    pair_total = sum(m * (m + 1) // 2 for m in range(depth))
    t_total = depth * (depth + 1) // 2
    vmem = pl.BlockSpec(memory_space=pltpu.VMEM)
    anywhere = pl.BlockSpec(memory_space=pl.ANY)
    line = 2**late
    early = depth - late
    products = sum((2 if m > 1 else 1) * (2 if depth - 1 - m in SPLIT else 1) for m in range(1, depth))
    copies = line + 2 * early + late + depth + products + 18 + 2 * (early - 3) + line - 1
    quarter = n // 8 * tile
    solved, mapped = pl.pallas_call(
        functools.partial(kernel, n, leaf),
        out_shape=(pltpu.VMEM((rows, samples), f32), pltpu.VMEM((tile, samples), f32)),
        in_specs=[pl.BlockSpec(memory_space=pltpu.HBM)] * 9,
        out_specs=(vmem, vmem),
        scratch_shapes=[
            pltpu.VMEM((rows, samples), bf16),
            pltpu.VMEM((rows, leaf), bf16),
            pltpu.VMEM((levels, rows, rank), f32),
            pltpu.VMEM((levels, rows, rank), f32),
            pltpu.VMEM((1, rows), f32),
            pltpu.VMEM((1, 1, tile), f32),
            pltpu.VMEM((tile, samples), bf16),
            pltpu.SMEM((n, n), jnp.int32),
            pltpu.SMEM((n, n), jnp.int32),
            pltpu.VMEM((depth * rank, rows), bf16),
            pltpu.VMEM((rows, depth * rank), bf16),
            pltpu.VMEM((pair_total, rank, rank), f32),
            pltpu.VMEM((pair_total, rank, rank), bf16),
            pltpu.VMEM((pair_total, rank, rank), bf16),
            pltpu.VMEM((2, depth, rank, half), f32),
            pltpu.VMEM((2, t_total, rank, half), bf16),
            pltpu.VMEM((t_total, rank, half), bf16),
            pltpu.VMEM((depth, 2, rank, half), bf16),
            pltpu.VMEM((rows, samples), bf16),
            pltpu.VMEM((depth * rank, samples), bf16),
            pltpu.VMEM((n, 1, 128), f32),
            pltpu.VMEM((n * tile, rows), bf16),
            pltpu.VMEM((2, 2, 2, quarter, half), f32),
            pltpu.VMEM((2, 4, quarter, samples), bf16),
            pltpu.VMEM((2, 4, quarter, samples), bf16),
            pltpu.VMEM((2, 2, 2, quarter, half), bf16),
            pltpu.VMEM((2, 2, 2, quarter, half), bf16),
            pltpu.VMEM((2, 2, quarter, half), bf16),
            pltpu.VMEM((2, 2, quarter, half), bf16),
            pltpu.VMEM((2, 2, quarter, half), bf16),
            pltpu.VMEM((2, 2, quarter, half), bf16),
            pltpu.VMEM((line, tile, samples), bf16),
            pltpu.VMEM((line, tile, samples), bf16),
            pltpu.SemaphoreType.DMA((SENDS,)),
            pltpu.SemaphoreType.DMA((copies,)),
            pltpu.SemaphoreType.DMA((2 * (levels - depth) + 9,)),
        ],
        compiler_params=pltpu.CompilerParams(
            collective_id=0, has_side_effects=True, vmem_limit_bytes=VMEM_LIMIT
        ),
    )(
        *(
            pltpu.with_memory_space_constraint(array, pltpu.HBM)
            for array in (
                residual_cols,
                leaf_inverse,
                basis_left,
                basis_right,
                point_pos.reshape(n, 1, rows),
                map_pos.reshape(1, 1, tile),
                prior_map,
                block_first,
                block_count,
            )
        )
    )
    return pl.pallas_call(
        deliver,
        out_shape=(
            jax.ShapeDtypeStruct((rows, samples), f32),
            jax.ShapeDtypeStruct((tile, samples), f32),
        ),
        in_specs=[anywhere] * 2,
        out_specs=(pl.BlockSpec(memory_space=pltpu.HBM),) * 2,
        scratch_shapes=[pltpu.SemaphoreType.DMA((PIECES + 1,))],
        compiler_params=pltpu.CompilerParams(vmem_limit_bytes=1024 * 1024),
    )(solved, mapped)


def solution(mesh):
    in_specs = (
        P(("groups", "pts"), None),
        P(("groups", "pts"), None),
        P(None, ("groups", "pts"), None),
        P(None, ("groups", "pts"), None),
        P(),
        P("pts"),
        P(("groups", "pts"), None),
        P(),
        P(),
    )
    out_specs = (P(("groups", "pts"), None), P(("groups", "pts"), None))
    return jax.shard_map(body, mesh=mesh, in_specs=in_specs, out_specs=out_specs, check_vma=False)
```

```python
import functools

import jax
import jax.numpy as jnp
from jax import lax
from jax.experimental import pallas as pl
from jax.experimental.pallas import tpu as pltpu
from jax.sharding import PartitionSpec as P

AMPLITUDE = 0.2
FAR = -1e6
PIECES = 2
TOGETHER = 4
SENDS = 14
VMEM_LIMIT = 50 * 1024 * 1024
f32 = jnp.float32
bf16 = jnp.bfloat16


def mm(a, b):
    return jnp.dot(a, b, preferred_element_type=f32)


def kernel(
    n,
    leaf,
    res_hbm,
    inv_hbm,
    bl_hbm,
    br_hbm,
    pp_hbm,
    mp_hbm,
    prior_hbm,
    first_hbm,
    count_hbm,
    xs,
    map_ref,
    res_ref,
    inv_ref,
    bl_ref,
    br_ref,
    pu,
    mp_ref,
    prior_ref,
    first_ref,
    count_ref,
    rth,
    lh,
    gf,
    gs,
    gr,
    tf,
    ts,
    tr,
    cbuf,
    co,
    ps,
    mpb,
    wts,
    acc,
    ms,
    mr,
    fs,
    fr,
    ss,
    sr,
    lt,
    lr,
    zs,
    zr,
    gz,
    gy,
    cown,
    po,
    send_sem,
    recv_sem,
    load_sem,
):
    rows, samples = res_ref.shape
    rank = bl_ref.shape[2]
    levels = bl_ref.shape[0]
    half = samples // 2
    depth = n.bit_length() - 1
    tile = prior_ref.shape[0]
    late = samples // rank
    early = depth - late
    me = lax.axis_index("pts")
    bits = [lax.rem(me // 2**k, 2) for k in range(depth)]
    par = bits[0]
    pool = [None] * send_sem.shape[0]
    arrivals = []
    sends = []

    def partner(mask):
        device = me
        for k in range(depth):
            if (mask >> k) & 1:
                device = device + 2**k * (1 - 2 * bits[k])
        return device

    def describe(src, dst, send, recv, mask):
        return pltpu.make_async_remote_copy(
            src_ref=src,
            dst_ref=dst,
            send_sem=send_sem.at[send],
            recv_sem=recv_sem.at[recv],
            device_id={"pts": partner(mask)},
            device_id_type=pl.DeviceIdType.MESH,
        )

    def remote_all(src, dst, value):
        recv = arrival()
        for v in (3, 1, 2):
            src[v] = value(v)
            remote(src.at[v], dst.at[v], flips(v), recv)
        view = pl.ds(1, 2**late - 1)
        return describe(src.at[view], dst.at[view], 0, recv, 1)

    def flips(v):
        return sum(((v >> (late - 1 - i)) & 1) * 2 ** (early + i) for i in range(late))

    def arrival():
        arrivals.append(len(arrivals))
        return arrivals[-1]

    def remote(src, dst, mask, recv=None):
        slot = len(sends) % (len(pool) - 1) + 1
        if pool[slot] is not None:
            pool[slot].wait_send()
        copy = describe(src, dst, slot, arrival() if recv is None else recv, mask)
        copy.start()
        pool[slot] = copy
        sends.append(copy)
        return copy

    loads = {}

    def load(name, src, dst):
        loads[name] = pltpu.make_async_copy(src, dst, load_sem.at[len(loads)])
        loads[name].start()

    load("inv", inv_hbm, inv_ref)
    load("res", res_hbm, res_ref)
    tree = pl.ds(0, depth)
    load("r", br_hbm.at[tree], br_ref.at[tree])
    load("l", bl_hbm.at[tree], bl_ref.at[tree])
    if levels > depth:
        own_levels = pl.ds(depth, levels - depth)
        load("own_r", br_hbm.at[own_levels], br_ref.at[own_levels])
        load("own_l", bl_hbm.at[own_levels], bl_ref.at[own_levels])

    barrier = pltpu.get_barrier_semaphore()
    for mask in range(1, n):
        pl.semaphore_signal(
            barrier, inc=1, device_id={"pts": partner(mask)}, device_id_type=pl.DeviceIdType.MESH
        )
    load("mp", mp_hbm, mp_ref)
    load("pp", pp_hbm.at[me], pu)
    load("first", first_hbm, first_ref)
    load("count", count_hbm, count_ref)
    load("prior", prior_hbm, prior_ref)

    pairs = [m * (m + 1) // 2 for m in range(depth)]
    g_off, t_off = [], []
    g_at = t_at = 0
    for k in range(depth):
        m = depth - 1 - k
        g_off.append(g_at)
        t_off.append(t_at)
        g_at += pairs[m]
        t_at += m + 1

    loads["inv"].wait()
    loads["res"].wait()
    for b in range(rows // leaf):
        view = slice(b * leaf, (b + 1) * leaf)
        xs[view, :] = mm(inv_ref[view, :], res_ref[view, :])
    loads["r"].wait()
    for l in range(depth - 1, -1, -1):
        rth[l * rank : (l + 1) * rank, :] = br_ref[l].astype(bf16).T
    loads["l"].wait()
    for l in range(depth - 1, -1, -1):
        lh[:, l * rank : (l + 1) * rank] = bl_ref[l].astype(bf16)
    for m in range(depth - 1, 0, -2):
        low = max(m - 1, 1)
        product = mm(rth[: m * rank, :], lh[:, low * rank : (m + 1) * rank])
        for i in range(m, low - 1, -1):
            start = sum(range(i + 1, depth))
            part = product[: i * rank, (i - low) * rank : (i - low + 1) * rank]
            part = part.reshape(i, rank, rank)
            gf[start : start + i] = part
            gs[start : start + i] = part.astype(bf16)
    for name in ("mp", "pp", "first", "count", "prior"):
        loads[name].wait()
    mpb[0] = jnp.zeros((1, 128), f32)
    mpb[0, :, :tile] = mp_ref[0]

    with jax.named_scope("barrier"):
        pl.semaphore_wait(barrier, n - 1)

    group = 2**early
    spots = []
    for first_mask in range(0, n, group):
        low = max(first_mask, 1)
        recv = arrival()
        for mask in range(low, first_mask + group):
            describe(mpb.at[0], mpb.at[mask], 0, recv, mask).start()
        view = mpb.at[pl.ds(low, first_mask + group - low)]
        spots.append(describe(view, view, 0, recv, 1))
    others = mpb.at[pl.ds(1, n - 1)]
    pool[0] = describe(others, others, 0, 0, 1)

    g_copies = {}

    def g_span(k, part):
        m = depth - 1 - k
        skip = late if k < early else 0
        if part == "head":
            return g_off[k] + skip, m - skip
        return g_off[k] + m, pairs[m] - m

    def g_send(k, part):
        start, size = g_span(k, part)
        if size > 0:
            span = pl.ds(start, size)
            g_copies[k, part] = remote(gs.at[span], gr.at[span], 2**k)

    def g_wait(k, part):
        if (k, part) in g_copies:
            g_copies.pop((k, part)).wait_recv()

    def g_next(k):
        start, size = g_span(k, "rest")
        if size == 0:
            return
        g_wait(k, "rest")
        total = gf[start : start + size] + gr[start : start + size].astype(f32)
        gf[g_off[k + 1] : g_off[k + 1] + size] = total
        gs[g_off[k + 1] : g_off[k + 1] + size] = total.astype(bf16)

    g_send(0, "rest")
    g_send(0, "head")

    total_rows = rows * n
    if levels > depth:
        loads["own_r"].wait()
        loads["own_l"].wait()
    for level in range(levels - 1, depth - 1, -1):
        size = total_rows // 2 ** (level + 1)
        count = rows // size
        projected = []
        for a in range(count):
            view = slice(a * size, (a + 1) * size)
            part = mm(br_ref[level, view, :].astype(bf16).T, xs[view, :].astype(bf16))
            projected.append(part.astype(bf16))
        for a in range(count):
            view = slice(a * size, (a + 1) * size)
            xs[view, :] += mm(bl_ref[level, view, :].astype(bf16), projected[a ^ 1])
    right = xs[...].astype(bf16)

    def project(low, high):
        part = mm(rth[low * rank : high * rank, :], right)
        for h in range(2):
            t_half = part[:, h * half : (h + 1) * half].reshape(high - low, rank, half)
            tf[h, low:high] = t_half
            ts[h, low:high] = t_half.astype(bf16)

    project(late, depth)

    top = depth - 1
    t_copies = {
        (0, "urgent"): [
            remote(ts.at[1 - par, pl.ds(late, depth - late)], tr.at[pl.ds(late, depth - late)], 1),
            remote(ts.at[par, top], cbuf.at[top, par], 1),
        ],
    }
    project(0, late)

    def combine(k, low, high):
        m = depth - 1 - k
        if high <= low:
            return
        count = high - low
        mine = ts[par, t_off[k] + m]
        theirs = tr[t_off[k] + m]
        g_mine = gs[g_off[k] + low : g_off[k] + high].reshape(count * rank, rank)
        g_theirs = gr[g_off[k] + low : g_off[k] + high].reshape(count * rank, rank)
        gained = mm(g_mine, theirs) + mm(g_theirs, mine)
        total = (
            tf[par, low:high]
            + tr[t_off[k] + low : t_off[k] + high].astype(f32)
            + gained.reshape(count, rank, half)
        )
        tf[par, low:high] = total
        ts[par, t_off[k + 1] + low : t_off[k + 1] + high] = total.astype(bf16)

    def t_send(k, low, high, name):
        span = pl.ds(t_off[k] + low, high - low)
        t_copies[k, name] = [remote(ts.at[par, span], tr.at[span], 2**k)]

    def t_wait(k, name):
        for copy in t_copies.pop((k, name), []):
            copy.wait_recv()

    forwards = {}

    def forward(k):
        m = depth - 1 - k
        forwards[m] = remote(tr.at[t_off[k] + m], cbuf.at[m, par], 1)

    def weights(place, core):
        if core == 1:
            with jax.named_scope(f"spot{place}"):
                spots[place].wait_recv()
        start = place * group + core
        own_u = pu[...] * (2.0 * leaf)

        def one(e):
            spot = 0
            other = 0
            for i in range(depth):
                bit = lax.rem(e // 2**i, 2)
                spot = spot + bit * 2 ** (depth - 1 - i)
                other = other + lax.rem(bit + bits[i], 2) * 2**i
            first = first_ref[other, me]
            last = first + count_ref[other, me]
            t_col = jnp.broadcast_to(mpb[e] * (2.0 * leaf), (128, 128)).T[:tile]
            base = pl.multiple_of(spot * tile, tile)
            for b in range(rows // leaf):
                u_row = own_u[:, b * leaf : (b + 1) * leaf]
                listed = jnp.logical_and(first <= b, b < last)
                u_row = jnp.where(listed, u_row, FAR)
                left = jnp.maximum(1.0 - jnp.abs(t_col - u_row), 0.0)
                square = left * left
                value = square * square * (5.0 * AMPLITUDE - 4.0 * AMPLITUDE * left)
                wts[pl.ds(base, tile), b * leaf : (b + 1) * leaf] = value.astype(bf16)

        def several(i, carry):
            for j in range(TOGETHER):
                one(start + 2 * (i * TOGETHER + j))
            return carry

        lax.fori_loop(0, group // 2 // TOGETHER, several, 0)

    quarter = n // 8 * tile
    half_rows = 4 * quarter
    sums = {}

    def map_first(s, factor, order):
        with jax.named_scope(f"mapfirst{s}{order[0]}"):
            low, count = min(order), len(order)
            rows_of = slice(half_rows + low * quarter, half_rows + (low + count) * quarter)
            part = mm(wts[rows_of, :], factor[...])
            ms[s, low : low + count] = part.astype(bf16).reshape(count, quarter, samples)
            for j in order:
                sums[s, j] = remote(ms.at[s, j], mr.at[s, j], 1)

    kept = {}

    def keep(s, j, factor):
        if (s, j) not in kept:
            low = j // 2 * 2
            part = mm(wts[low * quarter : (low + 2) * quarter, :], factor[...])
            kept[s, low], kept[s, low + 1] = part[:quarter], part[quarter:]
        part = kept[s, j]
        with jax.named_scope(f"first{s}{j}"):
            sums[s, j].wait_recv()
        part = part + mr[s, j].astype(f32)
        return [part[:, c * half : (c + 1) * half] for c in range(2)]

    def map_second(s, factor, order):
        def to_x(slot, value):
            fs[s, slot, 0] = value.astype(bf16)
            sums[s, "x", slot] = remote(fs.at[s, slot, 0], fr.at[s, slot, 0], 2)

        def to_y(slot, value):
            fs[s, slot, 1] = value.astype(bf16)
            sums[s, "y", slot] = remote(fs.at[s, slot, 1], fr.at[s, slot, 1], 4)

        for j in order:
            part = keep(s, j, factor)
            if j == 3:
                to_x(1, part[0])
                to_y(1, part[1])
            if j == 2:
                to_x(0, part[0])
                acc[s, 1, 1] = part[1]
            if j == 1:
                to_y(0, part[1])
                acc[s, 1, 0] = part[0]
            if j == 0:
                for c in range(2):
                    acc[s, 0, c] = part[c]

    def map_third_x(s):
        with jax.named_scope(f"third{s}"):
            sums[s, "x", 1].wait_recv()
        ss[s, 0] = (acc[s, 1, 0] + fr[s, 1, 0].astype(f32)).astype(bf16)
        sums[s, "xy"] = remote(ss.at[s, 0], sr.at[s, 0], 4)

    def map_third_y(s):
        with jax.named_scope(f"thirdb{s}"):
            sums[s, "y", 1].wait_recv()
        ss[s, 1] = (acc[s, 1, 1] + fr[s, 1, 1].astype(f32)).astype(bf16)
        sums[s, "yx"] = remote(ss.at[s, 1], sr.at[s, 1], 2)

    def map_fourth(s):
        with jax.named_scope(f"fourth{s}"):
            for name in ((s, "x", 0), (s, "y", 0), (s, "xy"), (s, "yx")):
                sums[name].wait_recv()
        size = quarter
        for c in range(2):
            acc[s, 0, c] += fr[s, 0, c].astype(f32) + sr[s, c].astype(f32)
        base = 0
        for k in range(3, early):
            size = size // 2
            for c in range(2):
                lt[s, c, base : base + size, :] = acc[s, 0, c, size : 2 * size, :].astype(bf16)
            view = pl.ds(base, size)
            copy = remote(lt.at[s, :, view], lr.at[s, :, view], 2**k)
            copy.wait_recv()
            for c in range(2):
                acc[s, 0, c, :size, :] += lr[s, c, base : base + size, :].astype(f32)
            base += size
        return jnp.concatenate([acc[s, 0, c, :size, :] for c in range(2)], axis=1)

    late_factor = lh.at[:, pl.ds(0, late * rank)]

    def urgent(k):
        m = depth - 1 - k
        with jax.named_scope(f"turgent{k}"):
            t_wait(k, "urgent")
        if k > 0:
            forward(k)
        if m > late:
            with jax.named_scope(f"ghead{k}"):
                g_wait(k, "head")
            combine(k, late, m)
            t_send(k + 1, late, m, "urgent")

    low_levels = pl.ds(0, late)

    def correct(k, theirs):
        g_mine = gs[g_off[k] : g_off[k] + late].reshape(late * rank, rank)
        return mm(g_mine, theirs).reshape(late, rank, half)

    def rest_send(k):
        m = depth - 1 - k
        theirs = tr[t_off[k] + m]
        if k == 0:
            away = tf[1 - par, low_levels] + correct(0, cbuf[top, 1 - par])
            ts[1 - par, low_levels] = away.astype(bf16)
            t_copies[0, "rest"] = [remote(ts.at[1 - par, low_levels], tr.at[low_levels], 1)]
            tf[par, low_levels] += correct(0, theirs)
        else:
            total = tf[par, low_levels]
            if k < early:
                total = total + correct(k, theirs)
                tf[par, low_levels] = total
            ts[par, pl.ds(t_off[k], late)] = total.astype(bf16)
            t_send(k, 0, late, "rest")

    def rest_wait(k):
        with jax.named_scope(f"trest{k}"):
            t_wait(k, "rest")
        tf[par, low_levels] += tr[pl.ds(t_off[k], late)].astype(f32)

    def factors(k):
        with jax.named_scope(f"gnext{k}"):
            g_next(k)
        g_send(k + 1, "head")

    with jax.named_scope("gnext0"):
        g_next(0)
    g_send(1, "head")
    urgent(0)
    g_send(1, "rest")
    rest_send(0)

    places = n // group
    near, far = range(places // 2), range(places // 2, places)
    for core in (1, 0):
        for place in near:
            weights(place, core)
    rest_wait(0)
    urgent(1)
    rest_send(1)
    for place in far:
        weights(place, 1)
    map_first(0, late_factor, (3, 2))
    map_first(0, late_factor, (1, 0))
    for place in far:
        weights(place, 0)
    for k in range(2, early):
        if k == early - 1:
            map_second(0, late_factor, (3, 2))
        factors(k - 1)
        g_send(k, "rest")
        urgent(k)
        rest_wait(k - 1)
        rest_send(k)

    mine_cols = pl.ds(pl.multiple_of(par * half, half), half)
    other_cols = pl.ds(pl.multiple_of((1 - par) * half, half), half)

    def own(m):
        return tr[t_off[depth - 1 - m] + m]

    def sibling(m):
        return cbuf[m, 1 - par]

    def finish(columns, parts):
        stacked = jnp.concatenate(parts, axis=0)
        ps[late * rank :, columns] = stacked
        co[:, columns] = (xs[:, columns] + mm(lh[:, late * rank :], stacked)).astype(bf16)

    map_second(0, late_factor, (1, 0))
    finish(mine_cols, [own(m) for m in range(late, depth)])
    with jax.named_scope("forwards"):
        for m in range(late, depth - 1):
            forwards[m].wait_recv()
    finish(other_cols, [sibling(m) for m in range(late, depth)])
    map_first(1, co, (3, 2))
    map_first(1, co, (1, 0))
    map_third_x(0)
    map_third_y(0)
    map_second(1, co, (3, 2))
    rest_wait(early - 1)
    rest_send(early)
    factors(early - 1)
    map_second(1, co, (1, 0))

    def late_step(k):
        with jax.named_scope(f"turgent{k}"):
            t_wait(k, "rest")
        forward(k)
        if k < depth - 1:
            with jax.named_scope(f"ghead{k}"):
                g_wait(k, "head")
            combine(k, 0, depth - 1 - k)
            t_send(k + 1, 0, depth - 1 - k, "rest")

    def gather(m):
        with jax.named_scope(f"gather{m}"):
            forwards[m].wait_recv()
        ps[m * rank : (m + 1) * rank, mine_cols] = own(m)
        ps[m * rank : (m + 1) * rank, other_cols] = sibling(m)

    map_third_x(1)
    late_step(early)
    map_third_y(1)
    last = ts.at[par, t_off[depth - 1]]
    last_copy = remote(last, cown.at[par], 1)
    plane = map_fourth(0).astype(bf16)
    factor_lines = remote_all(gz, gy, lambda v: plane[v * tile : (v + 1) * tile, :rank])
    gather(1)
    total = mm(plane[:, rank:], ps[rank : 2 * rank, :])
    total = map_fourth(1) + total
    lines = remote_all(zs, zr, lambda v: total[v * tile : (v + 1) * tile].astype(bf16))

    def settle(low, high):
        rows_of = slice(low * rank, high * rank)
        gained = mm(lh[:, rows_of], ps[rows_of, :])
        for l in range(low, high):
            view = slice(l * rank, (l + 1) * rank)
            rest_of = (bl_ref[l] - lh[:, view].astype(f32)).astype(bf16)
            gained = gained + mm(rest_of, ps[view, :])
        xs[...] += gained

    settle(1, depth)
    late_step(depth - 1)
    with jax.named_scope("last"):
        last_copy.wait_recv()
    po[:, mine_cols] = last[...]
    po[:, other_cols] = cown[1 - par]
    with jax.named_scope("factorlines"):
        factor_lines.wait_recv()
    near_factor = plane[:tile, :rank].astype(f32) + gy[2].astype(f32)
    far_factor = gy[1].astype(f32) + gy[3].astype(f32)
    gather(0)
    tail = mm(near_factor.astype(bf16), ps[:rank, :]) + mm(far_factor.astype(bf16), po[...])
    settle(0, 1)
    result = prior_ref[...].astype(f32) + total[:tile] + tail
    with jax.named_scope("lines"):
        lines.wait_recv()
    for v in range(1, 2**late):
        result = result + zr[v].astype(f32)
    map_ref[...] = result
    with jax.named_scope("end"):
        for copy in pool:
            copy.wait_send()
    assert len(arrivals) == recv_sem.shape[0], len(arrivals)


def deliver(solved_ref, mapped_ref, out_ref, map_ref, sems):
    piece = solved_ref.shape[0] // PIECES
    copies = [pltpu.make_async_copy(mapped_ref, map_ref, sems.at[PIECES])]
    for i in range(PIECES):
        view = pl.ds(i * piece, piece)
        copies.append(pltpu.make_async_copy(solved_ref.at[view], out_ref.at[view], sems.at[i]))
    for copy in copies:
        copy.start()
    for copy in copies:
        copy.wait()


def body(
    residual_cols,
    leaf_inverse,
    basis_left,
    basis_right,
    point_pos,
    map_pos,
    prior_map,
    block_first,
    block_count,
):
    rows, samples = residual_cols.shape
    leaf = leaf_inverse.shape[1]
    levels, _, rank = basis_left.shape
    n = lax.axis_size("pts")
    depth = n.bit_length() - 1
    tile = map_pos.shape[0]
    half = samples // 2
    late = samples // rank
    pair_total = sum(m * (m + 1) // 2 for m in range(depth))
    t_total = depth * (depth + 1) // 2
    vmem = pl.BlockSpec(memory_space=pltpu.VMEM)
    anywhere = pl.BlockSpec(memory_space=pl.ANY)
    line = 2**late
    early = depth - late
    copies = line + 4 * early + late + depth + 2 * (early + 7) + 3
    quarter = n // 8 * tile
    solved, mapped = pl.pallas_call(
        functools.partial(kernel, n, leaf),
        out_shape=(pltpu.VMEM((rows, samples), f32), pltpu.VMEM((tile, samples), f32)),
        in_specs=[pl.BlockSpec(memory_space=pltpu.HBM)] * 9,
        out_specs=(vmem, vmem),
        scratch_shapes=[
            pltpu.VMEM((rows, samples), bf16),
            pltpu.VMEM((rows, leaf), bf16),
            pltpu.VMEM((levels, rows, rank), f32),
            pltpu.VMEM((levels, rows, rank), f32),
            pltpu.VMEM((1, rows), f32),
            pltpu.VMEM((1, 1, tile), f32),
            pltpu.VMEM((tile, samples), bf16),
            pltpu.SMEM((n, n), jnp.int32),
            pltpu.SMEM((n, n), jnp.int32),
            pltpu.VMEM((depth * rank, rows), bf16),
            pltpu.VMEM((rows, depth * rank), bf16),
            pltpu.VMEM((pair_total, rank, rank), f32),
            pltpu.VMEM((pair_total, rank, rank), bf16),
            pltpu.VMEM((pair_total, rank, rank), bf16),
            pltpu.VMEM((2, depth, rank, half), f32),
            pltpu.VMEM((2, t_total, rank, half), bf16),
            pltpu.VMEM((t_total, rank, half), bf16),
            pltpu.VMEM((depth, 2, rank, half), bf16),
            pltpu.VMEM((rows, samples), bf16),
            pltpu.VMEM((depth * rank, samples), bf16),
            pltpu.VMEM((n, 1, 128), f32),
            pltpu.VMEM((n * tile, rows), bf16),
            pltpu.VMEM((2, 2, 2, quarter, half), f32),
            pltpu.VMEM((2, 4, quarter, samples), bf16),
            pltpu.VMEM((2, 4, quarter, samples), bf16),
            pltpu.VMEM((2, 2, 2, quarter, half), bf16),
            pltpu.VMEM((2, 2, 2, quarter, half), bf16),
            pltpu.VMEM((2, 2, quarter, half), bf16),
            pltpu.VMEM((2, 2, quarter, half), bf16),
            pltpu.VMEM((2, 2, quarter, half), bf16),
            pltpu.VMEM((2, 2, quarter, half), bf16),
            pltpu.VMEM((line, tile, samples), bf16),
            pltpu.VMEM((line, tile, samples), bf16),
            pltpu.VMEM((line, tile, rank), bf16),
            pltpu.VMEM((line, tile, rank), bf16),
            pltpu.VMEM((2, rank, half), bf16),
            pltpu.VMEM((rank, samples), bf16),
            pltpu.SemaphoreType.DMA((SENDS,)),
            pltpu.SemaphoreType.DMA((copies,)),
            pltpu.SemaphoreType.DMA((11 if levels > depth else 9,)),
        ],
        compiler_params=pltpu.CompilerParams(
            collective_id=0, has_side_effects=True, vmem_limit_bytes=VMEM_LIMIT
        ),
    )(
        *(
            pltpu.with_memory_space_constraint(array, pltpu.HBM)
            for array in (
                residual_cols,
                leaf_inverse,
                basis_left,
                basis_right,
                point_pos.reshape(n, 1, rows),
                map_pos.reshape(1, 1, tile),
                prior_map,
                block_first,
                block_count,
            )
        )
    )
    return pl.pallas_call(
        deliver,
        out_shape=(
            jax.ShapeDtypeStruct((rows, samples), f32),
            jax.ShapeDtypeStruct((tile, samples), f32),
        ),
        in_specs=[anywhere] * 2,
        out_specs=(pl.BlockSpec(memory_space=pltpu.HBM),) * 2,
        scratch_shapes=[pltpu.SemaphoreType.DMA((PIECES + 1,))],
        compiler_params=pltpu.CompilerParams(vmem_limit_bytes=1024 * 1024),
    )(solved, mapped)


def solution(mesh):
    in_specs = (
        P(("groups", "pts"), None),
        P(("groups", "pts"), None),
        P(None, ("groups", "pts"), None),
        P(None, ("groups", "pts"), None),
        P(),
        P("pts"),
        P(("groups", "pts"), None),
        P(),
        P(),
    )
    out_specs = (P(("groups", "pts"), None), P(("groups", "pts"), None))
    return jax.shard_map(body, mesh=mesh, in_specs=in_specs, out_specs=out_specs, check_vma=False)
```

```python
import functools

import jax
import jax.numpy as jnp
from jax import lax
from jax.experimental import pallas as pl
from jax.experimental.pallas import tpu as pltpu
from jax.sharding import PartitionSpec as P

AMPLITUDE = 0.2
FAR = -1e6
PIECES = 2
TOGETHER = 4
SENDS = 14
VMEM_LIMIT = 50 * 1024 * 1024
f32 = jnp.float32
bf16 = jnp.bfloat16


def mm(a, b):
    return jnp.dot(a, b, preferred_element_type=f32)


def kernel(
    n,
    leaf,
    res_hbm,
    inv_hbm,
    bl_hbm,
    br_hbm,
    pp_hbm,
    mp_hbm,
    prior_hbm,
    first_hbm,
    count_hbm,
    xs,
    map_ref,
    res_ref,
    inv_ref,
    bl_ref,
    br_ref,
    pu,
    mp_ref,
    prior_ref,
    first_ref,
    count_ref,
    rth,
    lh,
    gf,
    gs,
    gr,
    tf,
    ts,
    tr,
    cbuf,
    co,
    ps,
    mpb,
    wts,
    acc,
    ms,
    mr,
    fs,
    fr,
    ss,
    sr,
    lt,
    lr,
    zs,
    zr,
    gz,
    gy,
    cown,
    po,
    send_sem,
    recv_sem,
    load_sem,
):
    rows, samples = res_ref.shape
    rank = bl_ref.shape[2]
    levels = bl_ref.shape[0]
    half = samples // 2
    depth = n.bit_length() - 1
    tile = prior_ref.shape[0]
    late = samples // rank
    early = depth - late
    me = lax.axis_index("pts")
    bits = [lax.rem(me // 2**k, 2) for k in range(depth)]
    par = bits[0]
    pool = [None] * send_sem.shape[0]
    arrivals = []
    sends = []

    def partner(mask):
        device = me
        for k in range(depth):
            if (mask >> k) & 1:
                device = device + 2**k * (1 - 2 * bits[k])
        return device

    def describe(src, dst, send, recv, mask):
        return pltpu.make_async_remote_copy(
            src_ref=src,
            dst_ref=dst,
            send_sem=send_sem.at[send],
            recv_sem=recv_sem.at[recv],
            device_id={"pts": partner(mask) if isinstance(mask, int) else mask},
            device_id_type=pl.DeviceIdType.MESH,
        )

    def remote_all(src, dst, value, start=True):
        recv = arrival()
        copies = []
        count = 2**late
        for v in range(1, count):
            src[v] = value(v)
        here = me // 2**early
        for step in range(1, count):
            there = lax.rem(here + step, count)
            device = me + (there - here) * 2**early
            v = 0
            for i in range(late):
                differ = lax.rem(here // 2**i + there // 2**i, 2)
                v = v + differ * 2 ** (late - 1 - i)
            copies.append(remote(src.at[v], dst.at[v], device, recv, start))
        view = pl.ds(1, count - 1)
        return copies, describe(src.at[view], dst.at[view], 0, recv, 1)

    def arrival():
        arrivals.append(len(arrivals))
        return arrivals[-1]

    def remote(src, dst, mask, recv=None, start=True):
        slot = len(sends) % (len(pool) - 1) + 1
        if pool[slot] is not None:
            pool[slot].wait_send()
        copy = describe(src, dst, slot, arrival() if recv is None else recv, mask)
        if start:
            copy.start()
        pool[slot] = copy
        sends.append(copy)
        return copy

    loads = {}

    def load(name, src, dst):
        loads[name] = pltpu.make_async_copy(src, dst, load_sem.at[len(loads)])
        loads[name].start()

    load("inv", inv_hbm, inv_ref)
    load("res", res_hbm, res_ref)
    tree = pl.ds(0, depth)
    load("r", br_hbm.at[tree], br_ref.at[tree])
    load("l", bl_hbm.at[tree], bl_ref.at[tree])
    if levels > depth:
        own_levels = pl.ds(depth, levels - depth)
        load("own_r", br_hbm.at[own_levels], br_ref.at[own_levels])
        load("own_l", bl_hbm.at[own_levels], bl_ref.at[own_levels])

    barrier = pltpu.get_barrier_semaphore()
    for mask in range(1, n):
        pl.semaphore_signal(
            barrier, inc=1, device_id={"pts": partner(mask)}, device_id_type=pl.DeviceIdType.MESH
        )
    load("mp", mp_hbm, mp_ref)
    load("pp", pp_hbm.at[me], pu)
    load("first", first_hbm, first_ref)
    load("count", count_hbm, count_ref)
    load("prior", prior_hbm, prior_ref)

    pairs = [m * (m + 1) // 2 for m in range(depth)]
    g_off, t_off = [], []
    g_at = t_at = 0
    for k in range(depth):
        m = depth - 1 - k
        g_off.append(g_at)
        t_off.append(t_at)
        g_at += pairs[m]
        t_at += m + 1

    loads["inv"].wait()
    loads["res"].wait()
    for b in range(rows // leaf):
        view = slice(b * leaf, (b + 1) * leaf)
        xs[view, :] = mm(inv_ref[view, :], res_ref[view, :])
    loads["r"].wait()
    for l in range(depth - 1, -1, -1):
        rth[l * rank : (l + 1) * rank, :] = br_ref[l].astype(bf16).T
    loads["l"].wait()
    for l in range(depth - 1, -1, -1):
        lh[:, l * rank : (l + 1) * rank] = bl_ref[l].astype(bf16)
    for m in range(depth - 1, 0, -2):
        low = max(m - 1, 1)
        product = mm(rth[: m * rank, :], lh[:, low * rank : (m + 1) * rank])
        for i in range(m, low - 1, -1):
            start = sum(range(i + 1, depth))
            part = product[: i * rank, (i - low) * rank : (i - low + 1) * rank]
            part = part.reshape(i, rank, rank)
            gf[start : start + i] = part
            gs[start : start + i] = part.astype(bf16)
    for name in ("mp", "pp", "first", "count", "prior"):
        loads[name].wait()
    mpb[0] = jnp.zeros((1, 128), f32)
    mpb[0, :, :tile] = mp_ref[0]

    with jax.named_scope("barrier"):
        pl.semaphore_wait(barrier, n - 1)

    group = 2**early
    spots = []
    for first_mask in range(0, n, group):
        low = max(first_mask, 1)
        recv = arrival()
        for mask in range(low, first_mask + group):
            describe(mpb.at[0], mpb.at[mask], 0, recv, mask).start()
        view = mpb.at[pl.ds(low, first_mask + group - low)]
        spots.append(describe(view, view, 0, recv, 1))
    others = mpb.at[pl.ds(1, n - 1)]
    pool[0] = describe(others, others, 0, 0, 1)

    g_copies = {}

    def g_span(k, part):
        m = depth - 1 - k
        skip = late if k < early else 0
        if part == "head":
            return g_off[k] + skip, m - skip
        return g_off[k] + m, pairs[m] - m

    def g_send(k, part):
        start, size = g_span(k, part)
        if size > 0:
            span = pl.ds(start, size)
            g_copies[k, part] = remote(gs.at[span], gr.at[span], 2**k)

    def g_wait(k, part):
        if (k, part) in g_copies:
            g_copies.pop((k, part)).wait_recv()

    def g_next(k):
        start, size = g_span(k, "rest")
        if size == 0:
            return
        g_wait(k, "rest")
        total = gf[start : start + size] + gr[start : start + size].astype(f32)
        gf[g_off[k + 1] : g_off[k + 1] + size] = total
        gs[g_off[k + 1] : g_off[k + 1] + size] = total.astype(bf16)

    g_send(0, "rest")
    g_send(0, "head")

    total_rows = rows * n
    if levels > depth:
        loads["own_r"].wait()
        loads["own_l"].wait()
    for level in range(levels - 1, depth - 1, -1):
        size = total_rows // 2 ** (level + 1)
        count = rows // size
        projected = []
        for a in range(count):
            view = slice(a * size, (a + 1) * size)
            part = mm(br_ref[level, view, :].astype(bf16).T, xs[view, :].astype(bf16))
            projected.append(part.astype(bf16))
        for a in range(count):
            view = slice(a * size, (a + 1) * size)
            xs[view, :] += mm(bl_ref[level, view, :].astype(bf16), projected[a ^ 1])
    right = xs[...].astype(bf16)

    def project(low, high):
        part = mm(rth[low * rank : high * rank, :], right)
        for h in range(2):
            t_half = part[:, h * half : (h + 1) * half].reshape(high - low, rank, half)
            tf[h, low:high] = t_half
            ts[h, low:high] = t_half.astype(bf16)

    project(late, depth)

    top = depth - 1
    t_copies = {
        (0, "urgent"): [
            remote(ts.at[1 - par, pl.ds(late, depth - late)], tr.at[pl.ds(late, depth - late)], 1),
            remote(ts.at[par, top], cbuf.at[top, par], 1),
        ],
    }
    project(0, late)

    def combine(k, low, high):
        m = depth - 1 - k
        if high <= low:
            return
        count = high - low
        mine = ts[par, t_off[k] + m]
        theirs = tr[t_off[k] + m]
        g_mine = gs[g_off[k] + low : g_off[k] + high].reshape(count * rank, rank)
        g_theirs = gr[g_off[k] + low : g_off[k] + high].reshape(count * rank, rank)
        gained = mm(g_mine, theirs) + mm(g_theirs, mine)
        total = (
            tf[par, low:high]
            + tr[t_off[k] + low : t_off[k] + high].astype(f32)
            + gained.reshape(count, rank, half)
        )
        tf[par, low:high] = total
        ts[par, t_off[k + 1] + low : t_off[k + 1] + high] = total.astype(bf16)

    def t_send(k, low, high, name):
        span = pl.ds(t_off[k] + low, high - low)
        t_copies[k, name] = [remote(ts.at[par, span], tr.at[span], 2**k)]

    def t_wait(k, name):
        for copy in t_copies.pop((k, name), []):
            copy.wait_recv()

    forwards = {}

    def forward(k):
        m = depth - 1 - k
        forwards[m] = remote(tr.at[t_off[k] + m], cbuf.at[m, par], 1)

    def weights(place, core):
        if core == 1:
            with jax.named_scope(f"spot{place}"):
                spots[place].wait_recv()
        start = place * group + core
        own_u = pu[...] * (2.0 * leaf)

        def one(e):
            spot = 0
            other = 0
            for i in range(depth):
                bit = lax.rem(e // 2**i, 2)
                spot = spot + bit * 2 ** (depth - 1 - i)
                other = other + lax.rem(bit + bits[i], 2) * 2**i
            first = first_ref[other, me]
            last = first + count_ref[other, me]
            t_col = jnp.broadcast_to(mpb[e] * (2.0 * leaf), (128, 128)).T[:tile]
            base = pl.multiple_of(spot * tile, tile)
            for b in range(rows // leaf):
                u_row = own_u[:, b * leaf : (b + 1) * leaf]
                listed = jnp.logical_and(first <= b, b < last)
                u_row = jnp.where(listed, u_row, FAR)
                left = jnp.maximum(1.0 - jnp.abs(t_col - u_row), 0.0)
                square = left * left
                value = square * square * (5.0 * AMPLITUDE - 4.0 * AMPLITUDE * left)
                wts[pl.ds(base, tile), b * leaf : (b + 1) * leaf] = value.astype(bf16)

        def several(i, carry):
            for j in range(TOGETHER):
                one(start + 2 * (i * TOGETHER + j))
            return carry

        lax.fori_loop(0, group // 2 // TOGETHER, several, 0)

    quarter = n // 8 * tile
    half_rows = 4 * quarter
    sums = {}

    def map_first(s, factor, order):
        with jax.named_scope(f"mapfirst{s}{order[0]}"):
            low, count = min(order), len(order)
            rows_of = slice(half_rows + low * quarter, half_rows + (low + count) * quarter)
            part = mm(wts[rows_of, :], factor[...])
            ms[s, low : low + count] = part.astype(bf16).reshape(count, quarter, samples)
            for j in order:
                sums[s, j] = remote(ms.at[s, j], mr.at[s, j], 1)

    kept = {}

    def keep(s, j, factor):
        if (s, j) not in kept:
            low = j // 2 * 2
            part = mm(wts[low * quarter : (low + 2) * quarter, :], factor[...])
            kept[s, low], kept[s, low + 1] = part[:quarter], part[quarter:]
        part = kept[s, j]
        with jax.named_scope(f"first{s}{j}"):
            sums[s, j].wait_recv()
        part = part + mr[s, j].astype(f32)
        return [part[:, c * half : (c + 1) * half] for c in range(2)]

    def map_second(s, factor, order):
        def to_x(slot, value):
            fs[s, slot, 0] = value.astype(bf16)
            sums[s, "x", slot] = remote(fs.at[s, slot, 0], fr.at[s, slot, 0], 2)

        def to_y(slot, value):
            fs[s, slot, 1] = value.astype(bf16)
            sums[s, "y", slot] = remote(fs.at[s, slot, 1], fr.at[s, slot, 1], 4)

        for j in order:
            part = keep(s, j, factor)
            if j == 3:
                to_x(1, part[0])
                to_y(1, part[1])
            if j == 2:
                to_x(0, part[0])
                acc[s, 1, 1] = part[1]
            if j == 1:
                to_y(0, part[1])
                acc[s, 1, 0] = part[0]
            if j == 0:
                for c in range(2):
                    acc[s, 0, c] = part[c]

    def map_third_x(s):
        with jax.named_scope(f"third{s}"):
            sums[s, "x", 1].wait_recv()
        ss[s, 0] = (acc[s, 1, 0] + fr[s, 1, 0].astype(f32)).astype(bf16)
        sums[s, "xy"] = remote(ss.at[s, 0], sr.at[s, 0], 4)

    def map_third_y(s):
        with jax.named_scope(f"thirdb{s}"):
            sums[s, "y", 1].wait_recv()
        ss[s, 1] = (acc[s, 1, 1] + fr[s, 1, 1].astype(f32)).astype(bf16)
        sums[s, "yx"] = remote(ss.at[s, 1], sr.at[s, 1], 2)

    def map_fourth(s):
        with jax.named_scope(f"fourth{s}"):
            for name in ((s, "x", 0), (s, "y", 0), (s, "xy"), (s, "yx")):
                sums[name].wait_recv()
        size = quarter
        for c in range(2):
            acc[s, 0, c] += fr[s, 0, c].astype(f32) + sr[s, c].astype(f32)
        base = 0
        for k in range(3, early):
            size = size // 2
            for c in range(2):
                lt[s, c, base : base + size, :] = acc[s, 0, c, size : 2 * size, :].astype(bf16)
            view = pl.ds(base, size)
            copy = remote(lt.at[s, :, view], lr.at[s, :, view], 2**k)
            copy.wait_recv()
            for c in range(2):
                acc[s, 0, c, :size, :] += lr[s, c, base : base + size, :].astype(f32)
            base += size
        return jnp.concatenate([acc[s, 0, c, :size, :] for c in range(2)], axis=1)

    late_factor = lh.at[:, pl.ds(0, late * rank)]

    def urgent(k):
        m = depth - 1 - k
        with jax.named_scope(f"turgent{k}"):
            t_wait(k, "urgent")
        if k > 0:
            forward(k)
        if m > late:
            with jax.named_scope(f"ghead{k}"):
                g_wait(k, "head")
            combine(k, late, m)
            t_send(k + 1, late, m, "urgent")

    low_levels = pl.ds(0, late)

    def correct(k, theirs):
        g_mine = gs[g_off[k] : g_off[k] + late].reshape(late * rank, rank)
        return mm(g_mine, theirs).reshape(late, rank, half)

    def rest_send(k):
        m = depth - 1 - k
        theirs = tr[t_off[k] + m]
        if k == 0:
            away = tf[1 - par, low_levels] + correct(0, cbuf[top, 1 - par])
            ts[1 - par, low_levels] = away.astype(bf16)
            t_copies[0, "rest"] = [remote(ts.at[1 - par, low_levels], tr.at[low_levels], 1)]
            tf[par, low_levels] += correct(0, theirs)
        else:
            total = tf[par, low_levels]
            if k < early:
                total = total + correct(k, theirs)
                tf[par, low_levels] = total
            ts[par, pl.ds(t_off[k], late)] = total.astype(bf16)
            t_send(k, 0, late, "rest")

    def rest_wait(k):
        with jax.named_scope(f"trest{k}"):
            t_wait(k, "rest")
        tf[par, low_levels] += tr[pl.ds(t_off[k], late)].astype(f32)

    def factors(k):
        with jax.named_scope(f"gnext{k}"):
            g_next(k)
        g_send(k + 1, "head")

    with jax.named_scope("gnext0"):
        g_next(0)
    g_send(1, "head")
    urgent(0)
    g_send(1, "rest")
    rest_send(0)

    places = n // group
    near, far = range(places // 2), range(places // 2, places)
    for place in range(places - 1):
        weights(place, 1)
    for place in near:
        weights(place, 0)
    weights(places - 1, 1)
    rest_wait(0)
    urgent(1)
    rest_send(1)
    map_first(0, late_factor, (3, 2))
    map_first(0, late_factor, (1, 0))
    for place in far:
        weights(place, 0)
    for k in range(2, early):
        if k == early - 1:
            map_second(0, late_factor, (3, 2))
        factors(k - 1)
        g_send(k, "rest")
        urgent(k)
        rest_wait(k - 1)
        rest_send(k)

    mine_cols = pl.ds(pl.multiple_of(par * half, half), half)
    other_cols = pl.ds(pl.multiple_of((1 - par) * half, half), half)

    def own(m):
        return tr[t_off[depth - 1 - m] + m]

    def sibling(m):
        return cbuf[m, 1 - par]

    def finish(columns, parts):
        stacked = jnp.concatenate(parts, axis=0)
        ps[late * rank :, columns] = stacked
        co[:, columns] = (xs[:, columns] + mm(lh[:, late * rank :], stacked)).astype(bf16)

    map_second(0, late_factor, (1, 0))
    finish(mine_cols, [own(m) for m in range(late, depth)])
    with jax.named_scope("forwards"):
        for m in range(late, depth - 1):
            forwards[m].wait_recv()
    finish(other_cols, [sibling(m) for m in range(late, depth)])
    map_first(1, co, (3, 2))
    map_first(1, co, (1, 0))
    map_second(1, co, (3, 2))
    map_third_x(0)
    map_third_y(0)
    map_second(1, co, (1, 0))
    rest_wait(early - 1)
    rest_send(early)
    factors(early - 1)

    def late_step(k):
        with jax.named_scope(f"turgent{k}"):
            t_wait(k, "rest")
        forward(k)
        if k < depth - 1:
            with jax.named_scope(f"ghead{k}"):
                g_wait(k, "head")
            combine(k, 0, depth - 1 - k)
            t_send(k + 1, 0, depth - 1 - k, "rest")

    def gather(m):
        with jax.named_scope(f"gather{m}"):
            forwards[m].wait_recv()
        ps[m * rank : (m + 1) * rank, mine_cols] = own(m)
        ps[m * rank : (m + 1) * rank, other_cols] = sibling(m)

    map_third_x(1)
    map_third_y(1)
    late_step(early)
    last = ts.at[par, t_off[depth - 1]]
    last_copy = remote(last, cown.at[par], 1)
    plane = map_fourth(0).astype(bf16)
    _, factor_lines = remote_all(gz, gy, lambda v: plane[v * tile : (v + 1) * tile, :rank])
    gather(1)
    total = mm(plane[:, rank:], ps[rank : 2 * rank, :])
    total = map_fourth(1) + total
    line_copies, lines = remote_all(
        zs, zr, lambda v: total[v * tile : (v + 1) * tile].astype(bf16), start=False
    )

    def start_lines(core):
        @pl.when(par == core)
        def _():
            for copy in line_copies:
                copy.start()

    start_lines(0)

    def settle(low, high):
        rows_of = slice(low * rank, high * rank)
        gained = mm(lh[:, rows_of], ps[rows_of, :])
        for l in range(low, high):
            view = slice(l * rank, (l + 1) * rank)
            rest_of = (bl_ref[l] - lh[:, view].astype(f32)).astype(bf16)
            gained = gained + mm(rest_of, ps[view, :])
        xs[...] += gained

    settle(1, depth)
    late_step(depth - 1)
    start_lines(1)
    with jax.named_scope("last"):
        last_copy.wait_recv()
    po[:, mine_cols] = last[...]
    po[:, other_cols] = cown[1 - par]
    with jax.named_scope("factorlines"):
        factor_lines.wait_recv()
    near_factor = plane[:tile, :rank].astype(f32) + gy[2].astype(f32)
    far_factor = gy[1].astype(f32) + gy[3].astype(f32)
    gather(0)
    tail = mm(near_factor.astype(bf16), ps[:rank, :]) + mm(far_factor.astype(bf16), po[...])
    settle(0, 1)
    result = prior_ref[...].astype(f32) + total[:tile] + tail
    with jax.named_scope("lines"):
        lines.wait_recv()
    for v in range(1, 2**late):
        result = result + zr[v].astype(f32)
    map_ref[...] = result
    with jax.named_scope("end"):
        for copy in pool:
            copy.wait_send()
    assert len(arrivals) == recv_sem.shape[0], len(arrivals)


def deliver(solved_ref, mapped_ref, out_ref, map_ref, sems):
    piece = solved_ref.shape[0] // PIECES
    copies = [pltpu.make_async_copy(mapped_ref, map_ref, sems.at[PIECES])]
    for i in range(PIECES):
        view = pl.ds(i * piece, piece)
        copies.append(pltpu.make_async_copy(solved_ref.at[view], out_ref.at[view], sems.at[i]))
    for copy in copies:
        copy.start()
    for copy in copies:
        copy.wait()


def body(
    residual_cols,
    leaf_inverse,
    basis_left,
    basis_right,
    point_pos,
    map_pos,
    prior_map,
    block_first,
    block_count,
):
    rows, samples = residual_cols.shape
    leaf = leaf_inverse.shape[1]
    levels, _, rank = basis_left.shape
    n = lax.axis_size("pts")
    depth = n.bit_length() - 1
    tile = map_pos.shape[0]
    half = samples // 2
    late = samples // rank
    pair_total = sum(m * (m + 1) // 2 for m in range(depth))
    t_total = depth * (depth + 1) // 2
    vmem = pl.BlockSpec(memory_space=pltpu.VMEM)
    anywhere = pl.BlockSpec(memory_space=pl.ANY)
    line = 2**late
    early = depth - late
    copies = line + 4 * early + late + depth + 2 * (early + 7) + 3
    quarter = n // 8 * tile
    solved, mapped = pl.pallas_call(
        functools.partial(kernel, n, leaf),
        out_shape=(pltpu.VMEM((rows, samples), f32), pltpu.VMEM((tile, samples), f32)),
        in_specs=[pl.BlockSpec(memory_space=pltpu.HBM)] * 9,
        out_specs=(vmem, vmem),
        scratch_shapes=[
            pltpu.VMEM((rows, samples), bf16),
            pltpu.VMEM((rows, leaf), bf16),
            pltpu.VMEM((levels, rows, rank), f32),
            pltpu.VMEM((levels, rows, rank), f32),
            pltpu.VMEM((1, rows), f32),
            pltpu.VMEM((1, 1, tile), f32),
            pltpu.VMEM((tile, samples), bf16),
            pltpu.SMEM((n, n), jnp.int32),
            pltpu.SMEM((n, n), jnp.int32),
            pltpu.VMEM((depth * rank, rows), bf16),
            pltpu.VMEM((rows, depth * rank), bf16),
            pltpu.VMEM((pair_total, rank, rank), f32),
            pltpu.VMEM((pair_total, rank, rank), bf16),
            pltpu.VMEM((pair_total, rank, rank), bf16),
            pltpu.VMEM((2, depth, rank, half), f32),
            pltpu.VMEM((2, t_total, rank, half), bf16),
            pltpu.VMEM((t_total, rank, half), bf16),
            pltpu.VMEM((depth, 2, rank, half), bf16),
            pltpu.VMEM((rows, samples), bf16),
            pltpu.VMEM((depth * rank, samples), bf16),
            pltpu.VMEM((n, 1, 128), f32),
            pltpu.VMEM((n * tile, rows), bf16),
            pltpu.VMEM((2, 2, 2, quarter, half), f32),
            pltpu.VMEM((2, 4, quarter, samples), bf16),
            pltpu.VMEM((2, 4, quarter, samples), bf16),
            pltpu.VMEM((2, 2, 2, quarter, half), bf16),
            pltpu.VMEM((2, 2, 2, quarter, half), bf16),
            pltpu.VMEM((2, 2, quarter, half), bf16),
            pltpu.VMEM((2, 2, quarter, half), bf16),
            pltpu.VMEM((2, 2, quarter, half), bf16),
            pltpu.VMEM((2, 2, quarter, half), bf16),
            pltpu.VMEM((line, tile, samples), bf16),
            pltpu.VMEM((line, tile, samples), bf16),
            pltpu.VMEM((line, tile, rank), bf16),
            pltpu.VMEM((line, tile, rank), bf16),
            pltpu.VMEM((2, rank, half), bf16),
            pltpu.VMEM((rank, samples), bf16),
            pltpu.SemaphoreType.DMA((SENDS,)),
            pltpu.SemaphoreType.DMA((copies,)),
            pltpu.SemaphoreType.DMA((11 if levels > depth else 9,)),
        ],
        compiler_params=pltpu.CompilerParams(
            collective_id=0, has_side_effects=True, vmem_limit_bytes=VMEM_LIMIT
        ),
    )(
        *(
            pltpu.with_memory_space_constraint(array, pltpu.HBM)
            for array in (
                residual_cols,
                leaf_inverse,
                basis_left,
                basis_right,
                point_pos.reshape(n, 1, rows),
                map_pos.reshape(1, 1, tile),
                prior_map,
                block_first,
                block_count,
            )
        )
    )
    return pl.pallas_call(
        deliver,
        out_shape=(
            jax.ShapeDtypeStruct((rows, samples), f32),
            jax.ShapeDtypeStruct((tile, samples), f32),
        ),
        in_specs=[anywhere] * 2,
        out_specs=(pl.BlockSpec(memory_space=pltpu.HBM),) * 2,
        scratch_shapes=[pltpu.SemaphoreType.DMA((PIECES + 1,))],
        compiler_params=pltpu.CompilerParams(vmem_limit_bytes=1024 * 1024),
    )(solved, mapped)


def solution(mesh):
    in_specs = (
        P(("groups", "pts"), None),
        P(("groups", "pts"), None),
        P(None, ("groups", "pts"), None),
        P(None, ("groups", "pts"), None),
        P(),
        P("pts"),
        P(("groups", "pts"), None),
        P(),
        P(),
    )
    out_specs = (P(("groups", "pts"), None), P(("groups", "pts"), None))
    return jax.shard_map(body, mesh=mesh, in_specs=in_specs, out_specs=out_specs, check_vma=False)
```

```python
import functools

import jax
import jax.numpy as jnp
from jax import lax
from jax.experimental import pallas as pl
from jax.experimental.pallas import tpu as pltpu
from jax.sharding import PartitionSpec as P

AMPLITUDE = 0.2
FAR = -1e6
PIECES = 1
TOGETHER = 4
SENDS = 11
VMEM_LIMIT = 50 * 1024 * 1024
f32 = jnp.float32
bf16 = jnp.bfloat16


def mm(a, b):
    return jnp.dot(a, b, preferred_element_type=f32)


def kernel(
    n,
    leaf,
    res_hbm,
    inv_hbm,
    bl_hbm,
    br_hbm,
    pp_hbm,
    mp_hbm,
    prior_hbm,
    first_hbm,
    count_hbm,
    xs,
    map_ref,
    res_ref,
    inv_ref,
    bl_ref,
    br_ref,
    pu,
    mp_ref,
    prior_ref,
    first_ref,
    count_ref,
    rth,
    lh,
    gf,
    gs,
    gr,
    tf,
    ts,
    tr,
    cbuf,
    co,
    ps,
    mpb,
    wts,
    acc,
    ms,
    mr,
    fs,
    fr,
    ss,
    sr,
    lt,
    lr,
    zs,
    zr,
    gz,
    gy,
    cown,
    po,
    send_sem,
    recv_sem,
    load_sem,
):
    rows, samples = res_ref.shape
    rank = bl_ref.shape[2]
    levels = bl_ref.shape[0]
    half = samples // 2
    depth = n.bit_length() - 1
    tile = prior_ref.shape[0]
    late = samples // rank
    early = depth - late
    me = lax.axis_index("pts")
    bits = [lax.rem(me // 2**k, 2) for k in range(depth)]
    par = bits[0]
    pool = [None] * send_sem.shape[0]
    arrivals = []
    sends = []

    def partner(mask):
        device = me
        for k in range(depth):
            if (mask >> k) & 1:
                device = device + 2**k * (1 - 2 * bits[k])
        return device

    def describe(src, dst, send, recv, mask):
        return pltpu.make_async_remote_copy(
            src_ref=src,
            dst_ref=dst,
            send_sem=send_sem.at[send],
            recv_sem=recv_sem.at[recv],
            device_id={"pts": partner(mask) if isinstance(mask, int) else mask},
            device_id_type=pl.DeviceIdType.MESH,
        )

    def remote_all(src, dst, value, start=True):
        recv = arrival()
        copies = []
        count = 2**late
        for v in range(1, count):
            src[v] = value(v)
        here = me // 2**early
        for step in range(1, count):
            there = lax.rem(here + step, count)
            device = me + (there - here) * 2**early
            v = 0
            for i in range(late):
                differ = lax.rem(here // 2**i + there // 2**i, 2)
                v = v + differ * 2 ** (late - 1 - i)
            copies.append((there, remote(src.at[v], dst.at[v], device, recv, start)))
        view = pl.ds(1, count - 1)
        return copies, describe(src.at[view], dst.at[view], 0, recv, 1)

    def arrival():
        arrivals.append(len(arrivals))
        return arrivals[-1]

    def remote(src, dst, mask, recv=None, start=True):
        slot = len(sends) % (len(pool) - 1) + 1
        if pool[slot] is not None:
            pool[slot].wait_send()
        copy = describe(src, dst, slot, arrival() if recv is None else recv, mask)
        if start:
            copy.start()
        pool[slot] = copy
        sends.append(copy)
        return copy

    loads = {}

    def load(name, src, dst):
        loads[name] = pltpu.make_async_copy(src, dst, load_sem.at[len(loads)])
        loads[name].start()

    load("inv", inv_hbm, inv_ref)
    load("res", res_hbm, res_ref)
    tree = pl.ds(0, depth)
    load("r", br_hbm.at[tree], br_ref.at[tree])
    load("l", bl_hbm.at[tree], bl_ref.at[tree])
    if levels > depth:
        own_levels = pl.ds(depth, levels - depth)
        load("own_r", br_hbm.at[own_levels], br_ref.at[own_levels])
        load("own_l", bl_hbm.at[own_levels], bl_ref.at[own_levels])

    barrier = pltpu.get_barrier_semaphore()
    for mask in range(1, n):
        pl.semaphore_signal(
            barrier, inc=1, device_id={"pts": partner(mask)}, device_id_type=pl.DeviceIdType.MESH
        )
    load("mp", mp_hbm, mp_ref)
    load("pp", pp_hbm.at[me], pu)
    load("first", first_hbm, first_ref)
    load("count", count_hbm, count_ref)
    load("prior", prior_hbm, prior_ref)

    pairs = [m * (m + 1) // 2 for m in range(depth)]
    g_off, t_off = [], []
    g_at = t_at = 0
    for k in range(depth):
        m = depth - 1 - k
        g_off.append(g_at)
        t_off.append(t_at)
        g_at += pairs[m]
        t_at += m + 1

    loads["inv"].wait()
    loads["res"].wait()
    for b in range(rows // leaf):
        view = slice(b * leaf, (b + 1) * leaf)
        xs[view, :] = mm(inv_ref[view, :], res_ref[view, :])
    loads["r"].wait()
    for l in range(depth - 1, -1, -1):
        rth[l * rank : (l + 1) * rank, :] = br_ref[l].astype(bf16).T
    loads["l"].wait()
    for l in range(depth - 1, -1, -1):
        lh[:, l * rank : (l + 1) * rank] = bl_ref[l].astype(bf16)
    for m in range(depth - 1, 0, -2):
        low = max(m - 1, 1)
        product = mm(rth[: m * rank, :], lh[:, low * rank : (m + 1) * rank])
        for i in range(m, low - 1, -1):
            start = sum(range(i + 1, depth))
            part = product[: i * rank, (i - low) * rank : (i - low + 1) * rank]
            part = part.reshape(i, rank, rank)
            gf[start : start + i] = part
            gs[start : start + i] = part.astype(bf16)
    for name in ("mp", "pp", "first", "count", "prior"):
        loads[name].wait()
    mpb[0] = jnp.zeros((1, 128), f32)
    mpb[0, :, :tile] = mp_ref[0]

    with jax.named_scope("barrier"):
        pl.semaphore_wait(barrier, n - 1)

    group = 2**early
    spots = []
    for first_mask in range(0, n, group):
        low = max(first_mask, 1)
        recv = arrival()
        for mask in range(low, first_mask + group):
            describe(mpb.at[0], mpb.at[mask], 0, recv, mask).start()
        view = mpb.at[pl.ds(low, first_mask + group - low)]
        spots.append(describe(view, view, 0, recv, 1))
    others = mpb.at[pl.ds(1, n - 1)]
    pool[0] = describe(others, others, 0, 0, 1)

    g_copies = {}

    def g_span(k, part):
        m = depth - 1 - k
        skip = late if k < early else 0
        if part == "head":
            return g_off[k] + skip, m - skip
        return g_off[k] + m, pairs[m] - m

    def g_send(k, part):
        start, size = g_span(k, part)
        if size > 0:
            span = pl.ds(start, size)
            g_copies[k, part] = remote(gs.at[span], gr.at[span], 2**k)

    def g_wait(k, part):
        if (k, part) in g_copies:
            g_copies.pop((k, part)).wait_recv()

    def g_next(k):
        start, size = g_span(k, "rest")
        if size == 0:
            return
        g_wait(k, "rest")
        total = gf[start : start + size] + gr[start : start + size].astype(f32)
        gf[g_off[k + 1] : g_off[k + 1] + size] = total
        gs[g_off[k + 1] : g_off[k + 1] + size] = total.astype(bf16)

    g_send(0, "rest")
    g_send(0, "head")

    total_rows = rows * n
    if levels > depth:
        loads["own_r"].wait()
        loads["own_l"].wait()
    for level in range(levels - 1, depth - 1, -1):
        size = total_rows // 2 ** (level + 1)
        count = rows // size
        projected = []
        for a in range(count):
            view = slice(a * size, (a + 1) * size)
            part = mm(br_ref[level, view, :].astype(bf16).T, xs[view, :].astype(bf16))
            projected.append(part.astype(bf16))
        for a in range(count):
            view = slice(a * size, (a + 1) * size)
            xs[view, :] += mm(bl_ref[level, view, :].astype(bf16), projected[a ^ 1])
    right = xs[...].astype(bf16)

    def project(low, high):
        part = mm(rth[low * rank : high * rank, :], right)
        for h in range(2):
            t_half = part[:, h * half : (h + 1) * half].reshape(high - low, rank, half)
            tf[h, low:high] = t_half
            ts[h, low:high] = t_half.astype(bf16)

    project(late, depth)

    top = depth - 1
    t_copies = {
        (0, "urgent"): [
            remote(ts.at[1 - par, pl.ds(late, depth - late)], tr.at[pl.ds(late, depth - late)], 1),
            remote(ts.at[par, top], cbuf.at[top, par], 1),
        ],
    }
    project(0, late)

    def combine(k, low, high):
        m = depth - 1 - k
        if high <= low:
            return
        count = high - low
        mine = ts[par, t_off[k] + m]
        theirs = tr[t_off[k] + m]
        g_mine = gs[g_off[k] + low : g_off[k] + high].reshape(count * rank, rank)
        g_theirs = gr[g_off[k] + low : g_off[k] + high].reshape(count * rank, rank)
        gained = mm(g_mine, theirs) + mm(g_theirs, mine)
        total = (
            tf[par, low:high]
            + tr[t_off[k] + low : t_off[k] + high].astype(f32)
            + gained.reshape(count, rank, half)
        )
        tf[par, low:high] = total
        ts[par, t_off[k + 1] + low : t_off[k + 1] + high] = total.astype(bf16)

    def t_send(k, low, high, name):
        span = pl.ds(t_off[k] + low, high - low)
        t_copies[k, name] = [remote(ts.at[par, span], tr.at[span], 2**k)]

    def t_wait(k, name):
        for copy in t_copies.pop((k, name), []):
            copy.wait_recv()

    forwards = {}

    def forward(k):
        m = depth - 1 - k
        forwards[m] = remote(tr.at[t_off[k] + m], cbuf.at[m, par], 1)

    def weights(place, core):
        if core == 1:
            with jax.named_scope(f"spot{place}"):
                spots[place].wait_recv()
        start = place * group + core
        own_u = pu[...] * (2.0 * leaf)

        def one(e):
            spot = 0
            other = 0
            for i in range(depth):
                bit = lax.rem(e // 2**i, 2)
                spot = spot + bit * 2 ** (depth - 1 - i)
                other = other + lax.rem(bit + bits[i], 2) * 2**i
            first = first_ref[other, me]
            last = first + count_ref[other, me]
            t_col = jnp.broadcast_to(mpb[e] * (2.0 * leaf), (128, 128)).T[:tile]
            base = pl.multiple_of(spot * tile, tile)
            for b in range(rows // leaf):
                u_row = own_u[:, b * leaf : (b + 1) * leaf]
                listed = jnp.logical_and(first <= b, b < last)
                u_row = jnp.where(listed, u_row, FAR)
                left = jnp.maximum(1.0 - jnp.abs(t_col - u_row), 0.0)
                square = left * left
                value = square * square * (5.0 * AMPLITUDE - 4.0 * AMPLITUDE * left)
                wts[pl.ds(base, tile), b * leaf : (b + 1) * leaf] = value.astype(bf16)

        def several(i, carry):
            for j in range(TOGETHER):
                one(start + 2 * (i * TOGETHER + j))
            return carry

        lax.fori_loop(0, group // 2 // TOGETHER, several, 0)

    quarter = n // 8 * tile
    half_rows = 4 * quarter
    sums = {}

    def map_first(s, factor, order):
        with jax.named_scope(f"mapfirst{s}{order[0]}"):
            low, count = min(order), len(order)
            rows_of = slice(half_rows + low * quarter, half_rows + (low + count) * quarter)
            part = mm(wts[rows_of, :], factor[...])
            ms[s, low : low + count] = part.astype(bf16).reshape(count, quarter, samples)
            for j in order:
                sums[s, j] = remote(ms.at[s, j], mr.at[s, j], 1)

    kept = {}

    def keep(s, j, factor):
        if (s, j) not in kept:
            low = j // 2 * 2
            part = mm(wts[low * quarter : (low + 2) * quarter, :], factor[...])
            kept[s, low], kept[s, low + 1] = part[:quarter], part[quarter:]
        part = kept[s, j]
        with jax.named_scope(f"first{s}{j}"):
            sums[s, j].wait_recv()
        part = part + mr[s, j].astype(f32)
        return [part[:, c * half : (c + 1) * half] for c in range(2)]

    def map_second(s, factor, order):
        def to_x(slot, value):
            fs[s, slot, 0] = value.astype(bf16)
            sums[s, "x", slot] = remote(fs.at[s, slot, 0], fr.at[s, slot, 0], 2)

        def to_y(slot, value):
            fs[s, slot, 1] = value.astype(bf16)
            sums[s, "y", slot] = remote(fs.at[s, slot, 1], fr.at[s, slot, 1], 4)

        for j in order:
            part = keep(s, j, factor)
            if j == 3:
                to_x(1, part[0])
                to_y(1, part[1])
            if j == 2:
                to_x(0, part[0])
                acc[s, 1, 1] = part[1]
            if j == 1:
                to_y(0, part[1])
                acc[s, 1, 0] = part[0]
            if j == 0:
                for c in range(2):
                    acc[s, 0, c] = part[c]

    def map_third_x(s):
        with jax.named_scope(f"third{s}"):
            sums[s, "x", 1].wait_recv()
        ss[s, 0] = (acc[s, 1, 0] + fr[s, 1, 0].astype(f32)).astype(bf16)
        sums[s, "xy"] = remote(ss.at[s, 0], sr.at[s, 0], 4)

    def map_third_y(s):
        with jax.named_scope(f"thirdb{s}"):
            sums[s, "y", 1].wait_recv()
        ss[s, 1] = (acc[s, 1, 1] + fr[s, 1, 1].astype(f32)).astype(bf16)
        sums[s, "yx"] = remote(ss.at[s, 1], sr.at[s, 1], 2)

    def map_fourth(s):
        with jax.named_scope(f"fourth{s}"):
            for name in ((s, "x", 0), (s, "y", 0), (s, "xy"), (s, "yx")):
                sums[name].wait_recv()
        size = quarter
        for c in range(2):
            acc[s, 0, c] += fr[s, 0, c].astype(f32) + sr[s, c].astype(f32)
        base = 0
        for k in range(3, early):
            size = size // 2
            for c in range(2):
                lt[s, c, base : base + size, :] = acc[s, 0, c, size : 2 * size, :].astype(bf16)
            view = pl.ds(base, size)
            copy = remote(lt.at[s, :, view], lr.at[s, :, view], 2**k)
            copy.wait_recv()
            for c in range(2):
                acc[s, 0, c, :size, :] += lr[s, c, base : base + size, :].astype(f32)
            base += size
        return jnp.concatenate([acc[s, 0, c, :size, :] for c in range(2)], axis=1)

    late_factor = lh.at[:, pl.ds(0, late * rank)]

    def urgent(k):
        m = depth - 1 - k
        with jax.named_scope(f"turgent{k}"):
            t_wait(k, "urgent")
        if k > 0:
            forward(k)
        if m > late:
            with jax.named_scope(f"ghead{k}"):
                g_wait(k, "head")
            combine(k, late, m)
            t_send(k + 1, late, m, "urgent")

    low_levels = pl.ds(0, late)

    def correct(k, theirs):
        g_mine = gs[g_off[k] : g_off[k] + late].reshape(late * rank, rank)
        return mm(g_mine, theirs).reshape(late, rank, half)

    def rest_send(k):
        m = depth - 1 - k
        theirs = tr[t_off[k] + m]
        if k == 0:
            away = tf[1 - par, low_levels] + correct(0, cbuf[top, 1 - par])
            ts[1 - par, low_levels] = away.astype(bf16)
            t_copies[0, "rest"] = [remote(ts.at[1 - par, low_levels], tr.at[low_levels], 1)]
            tf[par, low_levels] += correct(0, theirs)
        else:
            total = tf[par, low_levels]
            if k < early:
                total = total + correct(k, theirs)
                tf[par, low_levels] = total
            ts[par, pl.ds(t_off[k], late)] = total.astype(bf16)
            t_send(k, 0, late, "rest")

    def rest_wait(k):
        with jax.named_scope(f"trest{k}"):
            t_wait(k, "rest")
        tf[par, low_levels] += tr[pl.ds(t_off[k], late)].astype(f32)

    def factors(k):
        with jax.named_scope(f"gnext{k}"):
            g_next(k)
        g_send(k + 1, "head")

    with jax.named_scope("gnext0"):
        g_next(0)
    g_send(1, "head")
    urgent(0)
    g_send(1, "rest")
    rest_send(0)

    places = n // group
    near, far = range(places // 2), range(places // 2, places)
    for place in range(places - 1):
        weights(place, 1)
    for place in near:
        weights(place, 0)
    weights(places - 1, 1)
    rest_wait(0)
    urgent(1)
    rest_send(1)
    map_first(0, late_factor, (3, 2))
    map_first(0, late_factor, (1, 0))
    for place in far:
        weights(place, 0)
    for k in range(2, early):
        if k == early - 1:
            map_second(0, late_factor, (3, 2))
        factors(k - 1)
        g_send(k, "rest")
        urgent(k)
        rest_wait(k - 1)
        rest_send(k)

    mine_cols = pl.ds(pl.multiple_of(par * half, half), half)
    other_cols = pl.ds(pl.multiple_of((1 - par) * half, half), half)

    def own(m):
        return tr[t_off[depth - 1 - m] + m]

    def sibling(m):
        return cbuf[m, 1 - par]

    def finish(columns, parts):
        stacked = jnp.concatenate(parts, axis=0)
        ps[late * rank :, columns] = stacked
        co[:, columns] = (xs[:, columns] + mm(lh[:, late * rank :], stacked)).astype(bf16)

    map_second(0, late_factor, (1, 0))
    finish(mine_cols, [own(m) for m in range(late, depth)])
    with jax.named_scope("forwards"):
        for m in range(late, depth - 1):
            forwards[m].wait_recv()
    finish(other_cols, [sibling(m) for m in range(late, depth)])
    map_first(1, co, (3, 2))
    map_first(1, co, (1, 0))
    map_second(1, co, (3, 2))
    map_third_x(0)
    map_third_y(0)
    map_second(1, co, (1, 0))
    rest_wait(early - 1)
    rest_send(early)
    factors(early - 1)

    def late_step(k):
        with jax.named_scope(f"turgent{k}"):
            t_wait(k, "rest")
        forward(k)
        if k < depth - 1:
            with jax.named_scope(f"ghead{k}"):
                g_wait(k, "head")
            combine(k, 0, depth - 1 - k)
            t_send(k + 1, 0, depth - 1 - k, "rest")

    def gather(m):
        with jax.named_scope(f"gather{m}"):
            forwards[m].wait_recv()
        ps[m * rank : (m + 1) * rank, mine_cols] = own(m)
        ps[m * rank : (m + 1) * rank, other_cols] = sibling(m)

    map_third_x(1)
    map_third_y(1)
    late_step(early)
    last = ts.at[par, t_off[depth - 1]]
    last_copy = remote(last, cown.at[par], 1)
    plane = map_fourth(0).astype(bf16)
    _, factor_lines = remote_all(gz, gy, lambda v: plane[v * tile : (v + 1) * tile, :rank])
    gather(1)
    total = mm(plane[:, rank:], ps[rank : 2 * rank, :])
    total = map_fourth(1) + total
    line_copies, lines = remote_all(
        zs, zr, lambda v: total[v * tile : (v + 1) * tile].astype(bf16), start=False
    )

    @pl.when(par == 0)
    def _():
        for _, copy in line_copies:
            copy.start()

    def second_lines(first_place):
        for there, copy in line_copies:
            chosen = there == 0 if first_place else there > 0
            pl.when(jnp.logical_and(par == 1, chosen))(copy.start)

    def settle(low, high):
        rows_of = slice(low * rank, high * rank)
        gained = mm(lh[:, rows_of], ps[rows_of, :])
        for l in range(low, high):
            view = slice(l * rank, (l + 1) * rank)
            rest_of = (bl_ref[l] - lh[:, view].astype(f32)).astype(bf16)
            gained = gained + mm(rest_of, ps[view, :])
        xs[...] += gained

    settle(1, depth)
    late_step(depth - 1)
    second_lines(True)
    with jax.named_scope("last"):
        last_copy.wait_recv()
    po[:, mine_cols] = last[...]
    po[:, other_cols] = cown[1 - par]
    with jax.named_scope("factorlines"):
        factor_lines.wait_recv()
    second_lines(False)
    near_factor = plane[:tile, :rank].astype(f32) + gy[2].astype(f32)
    far_factor = gy[1].astype(f32) + gy[3].astype(f32)
    gather(0)
    tail = mm(near_factor.astype(bf16), ps[:rank, :]) + mm(far_factor.astype(bf16), po[...])
    settle(0, 1)
    result = prior_ref[...].astype(f32) + total[:tile] + tail
    with jax.named_scope("lines"):
        lines.wait_recv()
    for v in range(1, 2**late):
        result = result + zr[v].astype(f32)
    map_ref[...] = result
    with jax.named_scope("end"):
        for copy in pool:
            copy.wait_send()
    assert len(arrivals) == recv_sem.shape[0], len(arrivals)


def deliver(solved_ref, mapped_ref, out_ref, map_ref, sems):
    piece = solved_ref.shape[0] // PIECES
    copies = [pltpu.make_async_copy(mapped_ref, map_ref, sems.at[PIECES])]
    for i in range(PIECES):
        view = pl.ds(i * piece, piece)
        copies.append(pltpu.make_async_copy(solved_ref.at[view], out_ref.at[view], sems.at[i]))
    for copy in copies:
        copy.start()
    for copy in copies:
        copy.wait()


def body(
    residual_cols,
    leaf_inverse,
    basis_left,
    basis_right,
    point_pos,
    map_pos,
    prior_map,
    block_first,
    block_count,
):
    rows, samples = residual_cols.shape
    leaf = leaf_inverse.shape[1]
    levels, _, rank = basis_left.shape
    n = lax.axis_size("pts")
    depth = n.bit_length() - 1
    tile = map_pos.shape[0]
    half = samples // 2
    late = samples // rank
    pair_total = sum(m * (m + 1) // 2 for m in range(depth))
    t_total = depth * (depth + 1) // 2
    vmem = pl.BlockSpec(memory_space=pltpu.VMEM)
    anywhere = pl.BlockSpec(memory_space=pl.ANY)
    line = 2**late
    early = depth - late
    copies = line + 4 * early + late + depth + 2 * (early + 7) + 3
    quarter = n // 8 * tile
    solved, mapped = pl.pallas_call(
        functools.partial(kernel, n, leaf),
        out_shape=(pltpu.VMEM((rows, samples), f32), pltpu.VMEM((tile, samples), f32)),
        in_specs=[pl.BlockSpec(memory_space=pltpu.HBM)] * 9,
        out_specs=(vmem, vmem),
        scratch_shapes=[
            pltpu.VMEM((rows, samples), bf16),
            pltpu.VMEM((rows, leaf), bf16),
            pltpu.VMEM((levels, rows, rank), f32),
            pltpu.VMEM((levels, rows, rank), f32),
            pltpu.VMEM((1, rows), f32),
            pltpu.VMEM((1, 1, tile), f32),
            pltpu.VMEM((tile, samples), bf16),
            pltpu.SMEM((n, n), jnp.int32),
            pltpu.SMEM((n, n), jnp.int32),
            pltpu.VMEM((depth * rank, rows), bf16),
            pltpu.VMEM((rows, depth * rank), bf16),
            pltpu.VMEM((pair_total, rank, rank), f32),
            pltpu.VMEM((pair_total, rank, rank), bf16),
            pltpu.VMEM((pair_total, rank, rank), bf16),
            pltpu.VMEM((2, depth, rank, half), f32),
            pltpu.VMEM((2, t_total, rank, half), bf16),
            pltpu.VMEM((t_total, rank, half), bf16),
            pltpu.VMEM((depth, 2, rank, half), bf16),
            pltpu.VMEM((rows, samples), bf16),
            pltpu.VMEM((depth * rank, samples), bf16),
            pltpu.VMEM((n, 1, 128), f32),
            pltpu.VMEM((n * tile, rows), bf16),
            pltpu.VMEM((2, 2, 2, quarter, half), f32),
            pltpu.VMEM((2, 4, quarter, samples), bf16),
            pltpu.VMEM((2, 4, quarter, samples), bf16),
            pltpu.VMEM((2, 2, 2, quarter, half), bf16),
            pltpu.VMEM((2, 2, 2, quarter, half), bf16),
            pltpu.VMEM((2, 2, quarter, half), bf16),
            pltpu.VMEM((2, 2, quarter, half), bf16),
            pltpu.VMEM((2, 2, quarter, half), bf16),
            pltpu.VMEM((2, 2, quarter, half), bf16),
            pltpu.VMEM((line, tile, samples), bf16),
            pltpu.VMEM((line, tile, samples), bf16),
            pltpu.VMEM((line, tile, rank), bf16),
            pltpu.VMEM((line, tile, rank), bf16),
            pltpu.VMEM((2, rank, half), bf16),
            pltpu.VMEM((rank, samples), bf16),
            pltpu.SemaphoreType.DMA((SENDS,)),
            pltpu.SemaphoreType.DMA((copies,)),
            pltpu.SemaphoreType.DMA((11 if levels > depth else 9,)),
        ],
        compiler_params=pltpu.CompilerParams(
            collective_id=0, has_side_effects=True, vmem_limit_bytes=VMEM_LIMIT
        ),
    )(
        *(
            pltpu.with_memory_space_constraint(array, pltpu.HBM)
            for array in (
                residual_cols,
                leaf_inverse,
                basis_left,
                basis_right,
                point_pos.reshape(n, 1, rows),
                map_pos.reshape(1, 1, tile),
                prior_map,
                block_first,
                block_count,
            )
        )
    )
    return pl.pallas_call(
        deliver,
        out_shape=(
            jax.ShapeDtypeStruct((rows, samples), f32),
            jax.ShapeDtypeStruct((tile, samples), f32),
        ),
        in_specs=[anywhere] * 2,
        out_specs=(pl.BlockSpec(memory_space=pltpu.HBM),) * 2,
        scratch_shapes=[pltpu.SemaphoreType.DMA((PIECES + 1,))],
        compiler_params=pltpu.CompilerParams(vmem_limit_bytes=1024 * 1024),
    )(solved, mapped)


def solution(mesh):
    in_specs = (
        P(("groups", "pts"), None),
        P(("groups", "pts"), None),
        P(None, ("groups", "pts"), None),
        P(None, ("groups", "pts"), None),
        P(),
        P("pts"),
        P(("groups", "pts"), None),
        P(),
        P(),
    )
    out_specs = (P(("groups", "pts"), None), P(("groups", "pts"), None))
    return jax.shard_map(body, mesh=mesh, in_specs=in_specs, out_specs=out_specs, check_vma=False)
```
